32 devices in a mesh: gz: 8 (over y, x, core), gy: 4 (over z).
Axes of the slice: x: 2, y: 2, z: 4, core: 2. Of those that a mesh axis runs over, the one named last changes fastest.
Arguments:
- concentration_components: float32 [8, 64, 32, 512], P(None, 'gz', 'gy'), may hold values from -6 to 6
- thermal_state: float32 [64, 32, 512], P('gz', 'gy'), may hold values from 0.8 to 2
- spreading_coefficients: float32 [8], replicated, may hold values from 0.1 to 0.8
- frequency_prefactor: float32 [8], replicated, may hold values from 1 to 6
- barrier_heights: float32 [8], replicated, may hold values from 0.5 to 3
- stoichiometric_matrix: float32 [8, 8], replicated, may hold values from 0 to 0.4
- basis_matrix_east: float32 [512, 128], replicated, may hold values from -0.25 to 0.25
- basis_matrix_north: float32 [32, 32], replicated, may hold values from -1 to 1
- basis_matrix_upward: float32 [64, 32], replicated, may hold values from -0.75 to 0.75
Outputs:
- species_next: float32 [8, 64, 32, 512], P(None, 'gz', 'gy')
- core_block: float32 [8, 32, 32, 128], P(None, None, 'gz')
The draws below stay inside these ranges and needn't reach their ends.
All inputs are finite; a program needn't handle non-finite values.
Results may differ from the reference program's by a relative error of at most 0.00007.
Values sent between devices are 32-bit elements; how exact they have to be, the bound alone decides.
A program may use at most 64 MiB of HBM per device.

```python
import math
import jax
import jax.numpy as jnp
from jax import lax

S = 8
RX = 128
RY = 32
RZ = 32
MESH_POINTS_EAST = 512
MESH_POINTS_UP = 64
MESH_POINTS_NORTH = 32


def levels(own_key, dims, split, least, high):
    def one(dim, blocks):
        heights = jax.random.uniform(jax.random.fold_in(jax.random.fold_in(own_key, 6), dim), (blocks,), jnp.float32, least / len(split), high / len(split))
        return jnp.repeat(jnp.exp(heights), dims[dim] // blocks).reshape((-1,) + (1,) * (len(dims) - dim - 1))

    factor_of = one(*split[0])
    for cut in split[1:]:
        factor_of = factor_of * one(*cut)
    return factor_of


def bell_draw(rng, shape, scale, most, shards=(), held_as=jnp.bfloat16):
    factor_of = levels(rng, shape, shards, -0.22, 0.18) if shards else 1.0
    drawn = jax.random.normal(rng, shape, jnp.float32) * scale * factor_of
    return jnp.minimum(jnp.maximum(drawn, -most), most).astype(held_as)


def setup_inputs(seed: int = 0) -> dict:
    keys = jax.random.split(jax.random.key(seed), 10)
    concentration_components = bell_draw(keys[0], (S, MESH_POINTS_UP, MESH_POINTS_NORTH, MESH_POINTS_EAST), 1.0, 6.0, ((1, 8), (2, 4)), jnp.float32)
    thermal_state = jnp.clip(0.8 + 1.2 * jax.random.uniform(keys[1], (MESH_POINTS_UP, MESH_POINTS_NORTH, MESH_POINTS_EAST), jnp.float32) ** levels(keys[1], (MESH_POINTS_UP, MESH_POINTS_NORTH, MESH_POINTS_EAST), ((0, 8), (1, 4)), -0.2, 0.2), 0.8, 2.0)
    spreading_coefficients = jnp.clip(jnp.exp(jax.random.uniform(keys[2], (S,), jnp.float32, math.log(0.1), math.log(0.8))), 0.1, 0.8)
    frequency_prefactor = jnp.clip(jnp.exp(jax.random.uniform(keys[3], (S,), jnp.float32, math.log(1.0), math.log(6.0))), 1.0, 6.0)
    barrier_heights = jnp.clip(jnp.exp(jax.random.uniform(keys[4], (S,), jnp.float32, math.log(0.5), math.log(3.0))), 0.5, 3.0)
    stoichiometric_matrix = jnp.clip(jax.random.uniform(keys[5], (S, S), jnp.float32, 0.0, 0.4), 0.0, 0.4)
    basis_matrix_east = bell_draw(keys[6], (MESH_POINTS_EAST, RX), MESH_POINTS_EAST ** -0.5, 0.25, (), jnp.float32)
    basis_matrix_north = bell_draw(keys[7], (MESH_POINTS_NORTH, RY), MESH_POINTS_NORTH ** -0.5, 1.0, (), jnp.float32)
    basis_matrix_upward = bell_draw(keys[8], (MESH_POINTS_UP, RZ), MESH_POINTS_UP ** -0.5, 0.75, (), jnp.float32)
    return dict(concentration_components=concentration_components, thermal_state=thermal_state, spreading_coefficients=spreading_coefficients, frequency_prefactor=frequency_prefactor, barrier_heights=barrier_heights, stoichiometric_matrix=stoichiometric_matrix, basis_matrix_east=basis_matrix_east, basis_matrix_north=basis_matrix_north, basis_matrix_upward=basis_matrix_upward)


time_step = 0.1


def stencil(region, dimension, length):
    shifted = [lax.slice_in_dim(region, offset, offset + length, axis=dimension) for offset in range(5)]
    return (-shifted[0] + 16.0 * shifted[1] - 30.0 * shifted[2] + 16.0 * shifted[3] - shifted[4]) / 12.0


def laplace(values):
    padded = jnp.pad(values, 2)
    cells_deep, cells_wide, cells_long = values.shape
    along_depth = stencil(padded[:, 2:2 + cells_wide, 2:2 + cells_long], 0, cells_deep)
    along_width = stencil(padded[2:2 + cells_deep, :, 2:2 + cells_long], 1, cells_wide)
    along_length = stencil(padded[2:2 + cells_deep, 2:2 + cells_wide, :], 2, cells_long)
    return along_depth + along_width + along_length


def thermal_speed_law(thermal_state, frequency_prefactor, barrier_heights):
    return frequency_prefactor[:, None, None, None] * jnp.exp(-barrier_heights[:, None, None, None] / thermal_state[None])


def tendency(values, conversion_speed_map, spreading_coefficients, stoichiometric_matrix):
    turnover = conversion_speed_map * values
    source = jnp.einsum('st,tzyx->szyx', stoichiometric_matrix, turnover, precision=lax.Precision.HIGHEST) - turnover
    diffusion = lax.map(lambda member: member[1] * laplace(member[0]), (values, spreading_coefficients))
    return diffusion + source


def reference(concentration_components, thermal_state, spreading_coefficients, frequency_prefactor, barrier_heights, stoichiometric_matrix, basis_matrix_east, basis_matrix_north, basis_matrix_upward):
    conversion_speed_map = thermal_speed_law(thermal_state, frequency_prefactor, barrier_heights)
    halfway = concentration_components + time_step * tendency(concentration_components, conversion_speed_map, spreading_coefficients, stoichiometric_matrix)
    species_next = 0.5 * (concentration_components + halfway + time_step * tendency(halfway, conversion_speed_map, spreading_coefficients, stoichiometric_matrix))
    projected_first = jnp.einsum('szyx,xr->szyr', species_next, basis_matrix_east, precision=lax.Precision.HIGHEST)
    projected_second = jnp.einsum('szyr,yq->szqr', projected_first, basis_matrix_north, precision=lax.Precision.HIGHEST)
    core_block = jnp.einsum('szqr,zp->spqr', projected_second, basis_matrix_upward, precision=lax.Precision.HIGHEST)
    return species_next, core_block
```

```python
import functools

import jax
import jax.numpy as jnp
from jax import lax
from jax.experimental import pallas as pl
from jax.experimental.pallas import tpu as pltpu
from jax.sharding import PartitionSpec as P

time_step = 0.1
chunk_ranks = 8
MESH = pl.DeviceIdType.MESH
HIGHEST = lax.Precision.HIGHEST
f32 = jnp.float32


def iota(shape, dim):
    return lax.broadcasted_iota(jnp.int32, shape, dim)


def dot(a, b, dims=(((1,), (0,)), ((), ()))):
    return lax.dot_general(a, b, dims, precision=HIGHEST, preferred_element_type=f32)


def split(x):
    top = x.astype(jnp.bfloat16)
    return top, (x - top.astype(f32)).astype(jnp.bfloat16)


def dot3(a, b):
    (a1, a2), (b1, b2) = a, b
    small = jnp.dot(a1, b2, preferred_element_type=f32)
    small += jnp.dot(a2, b1, preferred_element_type=f32)
    return small + jnp.dot(a1, b1, preferred_element_type=f32)


def kernel(ngz, ngy, fused, *refs):
    (
        u_hbm,
        t_hbm,
        d_hbm,
        a_hbm,
        b_hbm,
        m_hbm,
        e_hbm,
        n_hbm,
        up_hbm,
        next_hbm,
    ) = refs[:10]
    rest = refs[10:]
    if fused:
        core_hbm, rest = rest[0], rest[1:]
    (
        field,
        half,
        rate,
        result,
        thermal,
        zhalo,
        yhalo,
        ysend,
        d_ref,
        a_ref,
        b_ref,
        m_ref,
        load_sem,
        halo_send,
        halo_recv,
    ) = rest[:15]
    if fused:
        (
            east,
            n_ref,
            up_ref,
            first,
            gathered,
            second,
            slabs,
            east_parts,
            up_parts,
            north_parts,
            first_send,
            first_recv,
            second_send,
            second_recv,
            third_send,
            third_recv,
        ) = rest[15:]

    species, depth, width, length = u_hbm.shape
    gz = lax.axis_index("gz")
    gy = lax.axis_index("gy")
    has = [gz > 0, gz < ngz - 1, gy > 0, gy < ngy - 1]
    names = ["gz", "gz", "gy", "gy"]
    other = [gz - 1, gz + 1, gy - 1, gy + 1]

    load_u = pltpu.make_async_copy(u_hbm, field.at[:, 2 : 2 + depth], load_sem.at[0])
    load_t = pltpu.make_async_copy(t_hbm, thermal, load_sem.at[1])
    small = [
        pltpu.make_async_copy(src, dst, load_sem.at[5 + i])
        for i, (src, dst) in enumerate(
            ((d_hbm, d_ref), (a_hbm, a_ref), (b_hbm, b_ref), (m_hbm, m_ref))
        )
    ]
    load_u.start()
    for copy in small:
        copy.start()
    load_t.start()
    if fused:
        load_e = pltpu.make_async_copy(e_hbm, east, load_sem.at[2])
        load_n = pltpu.make_async_copy(n_hbm, n_ref, load_sem.at[9])
        load_up = pltpu.make_async_copy(up_hbm, up_ref, load_sem.at[10])
        for copy in (load_e, load_n, load_up):
            copy.start()

    barrier = pltpu.get_barrier_semaphore()
    if fused:
        for k in range(1, ngz):
            pl.semaphore_signal(
                barrier, inc=1, device_id={"gz": lax.rem(gz + k, ngz)}, device_id_type=MESH
            )
        for k in range(1, ngy):
            pl.semaphore_signal(
                barrier, inc=1, device_id={"gy": lax.rem(gy + k, ngy)}, device_id_type=MESH
            )
    partners = () if fused else (0, 1, 2, 3)
    for side in partners:

        @pl.when(has[side])
        def _(side=side):
            pl.semaphore_signal(
                barrier, inc=1, device_id={names[side]: other[side]}, device_id_type=MESH
            )

    zeros = jnp.zeros((species, 2, width, length), f32)
    for buffer in (field, half):
        buffer[:, 0:2] = zeros
        buffer[:, 2 + depth : 4 + depth] = zeros
    for side in range(2):

        @pl.when(jnp.logical_not(has[side]))
        def _(side=side):
            for stage in range(2):
                zhalo[stage, side] = zeros

        @pl.when(jnp.logical_not(has[2 + side]))
        def _(side=side):
            for stage in range(2):
                yhalo[stage, side] = jnp.zeros(yhalo.shape[2:], f32)

    row = iota((width, length), 0)
    lane = iota((width, length), 1)
    per = width // 2
    packs = depth // per

    def weight(s, stage):
        return d_ref[s] * (time_step / 12.0 * (0.5 if stage else 1.0))

    turns = 2 if species % 2 == 0 else 1

    def each_species(step, start=0, stop=species):
        def body(i, carry):
            step(lax.rem(i * turns, species) + i * turns // species)
            return carry

        lax.fori_loop(start, stop, body, 0)

    def pack_rows(source, stage, s):
        first_gain = jnp.where(row == 0, 16.0, 0.0)
        last_gain = jnp.where(row == width - 1, 16.0, 0.0)

        k = weight(s, stage)
        for group in range(packs):
            up = jnp.zeros((width, length), f32)
            down = jnp.zeros((width, length), f32)
            for i in range(per):
                v = source[s, 2 + group * per + i] * k
                rising = first_gain * pltpu.roll(v, 1, 0) - pltpu.roll(v, 2, 0)
                falling = last_gain * pltpu.roll(v, width - 1, 0) - pltpu.roll(
                    v, width - 2, 0
                )
                here = jnp.logical_and(row >= 2 * i, row < 2 * i + 2)
                if i:
                    rising = pltpu.roll(rising, 2 * i, 0)
                falling = pltpu.roll(falling, (2 * i + 2) % width, 0) if i < per - 1 else falling
                up = jnp.where(here, rising, up)
                down = jnp.where(here, falling, down)
            ysend[stage, 0, s, group] = down
            ysend[stage, 1, s, group] = up

    def halo_copy(stage, side, s):
        if side < 2:
            start = 0 if side == 0 else depth - 2
            if stage == 0:
                src = u_hbm.at[s, start : start + 2]
            else:
                src = half.at[s, 2 + start : 4 + start]
            dst = zhalo.at[stage, 1 - side, s]
        else:
            src = ysend.at[stage, side - 2, s]
            dst = yhalo.at[stage, 3 - side, s]
        opposite = side ^ 1
        return pltpu.make_async_remote_copy(
            src_ref=src,
            dst_ref=dst,
            send_sem=halo_send.at[stage, side, s],
            recv_sem=halo_recv.at[stage, opposite, s],
            device_id={names[side]: other[side]},
            device_id_type=MESH,
        )

    def arrived(stage, side, s):
        dst = zhalo.at[stage, side, s] if side < 2 else yhalo.at[stage, side - 2, s]
        return pltpu.make_async_remote_copy(
            src_ref=dst,
            dst_ref=dst,
            send_sem=halo_send.at[stage, side, s],
            recv_sem=halo_recv.at[stage, side, s],
            device_id={names[side]: other[side]},
            device_id_type=MESH,
        )

    def send_halos(stage, sides, s):
        for side in sides:

            @pl.when(has[side])
            def _(side=side):
                halo_copy(stage, side, s).start()

    def wait_halos(stage, s):
        for side in range(4):

            @pl.when(has[side])
            def _(side=side):
                arrived(stage, side, s).wait_recv()

    def local_pass(source, target, stage):
        offset = 0 if stage else 2
        gain = 0.5 if stage else 1.0

        def body(z, carry):
            for s in range(species):
                c = source[s, z + 2]
                near = source[s, z + 1] + source[s, z + 3]
                far = source[s, z] + source[s, z + 4]
                near += jnp.where(row >= 1, pltpu.roll(c, 1, 0), 0.0)
                near += jnp.where(row < width - 1, pltpu.roll(c, width - 1, 0), 0.0)
                far += jnp.where(row >= 2, pltpu.roll(c, 2, 0), 0.0)
                far += jnp.where(row < width - 2, pltpu.roll(c, width - 2, 0), 0.0)
                near += jnp.where(lane >= 1, pltpu.roll(c, 1, 1), 0.0)
                near += jnp.where(lane < length - 1, pltpu.roll(c, length - 1, 1), 0.0)
                far += jnp.where(lane >= 2, pltpu.roll(c, 2, 1), 0.0)
                far += jnp.where(lane < length - 2, pltpu.roll(c, length - 2, 1), 0.0)
                total = weight(s, stage) * (16.0 * near - far - 90.0 * c)
                if stage:
                    total += 0.5 * (c + field[s, z + 2])
                else:
                    total += c
                target[s, z + offset] = total
            for tile in range(0, length, 128):
                part = pl.ds(tile, 128)
                turnover = [
                    (rate[t, z, :, part] * source[t, z + 2, :, part]) * (gain * time_step)
                    for t in range(species)
                ]
                for s in range(species):
                    total = target[s, z + offset, :, part] - turnover[s]
                    for t in range(species):
                        total += m_ref[s, t] * turnover[t]
                    target[s, z + offset, :, part] = total
            return carry

        lax.fori_loop(0, depth, body, 0)

    def fix(target, stage, s):
        offset = 0 if stage else 2

        k = weight(s, stage)
        add = {}
        below, above = zhalo[stage, 0, s], zhalo[stage, 1, s]
        add[0] = k * (16.0 * below[1] - below[0])
        add[1] = -k * below[1]
        add[depth - 1] = k * (16.0 * above[0] - above[1])
        add[depth - 2] = -k * above[0]
        for group in range(packs):
            low, high = yhalo[stage, 0, s, group], yhalo[stage, 1, s, group]
            for i in range(per):
                z = group * per + i
                shift = (width - 2 * i) % width
                value = target[s, z + offset]
                value += jnp.where(row < 2, pltpu.roll(low, shift, 0) if shift else low, 0.0)
                shift = (2 * width - 2 - 2 * i) % width
                value += jnp.where(
                    row >= width - 2, pltpu.roll(high, shift, 0) if shift else high, 0.0
                )
                if z in add:
                    value += add[z]
                target[s, z + offset] = value

    for copy in small:
        copy.wait()
    load_u.wait()
    each_species(lambda s: pack_rows(field, 0, s))
    if fused:
        pl.semaphore_wait(barrier, ngz + ngy - 2)
    for side in partners:

        @pl.when(has[side])
        def _():
            pl.semaphore_wait(barrier, 1)

    each_species(lambda s: send_halos(0, (2, 3, 0, 1), s))

    load_t.wait()

    def rates(z, carry):
        inverse = 1.0 / thermal[z]
        for s in range(species):
            rate[s, z] = a_ref[s] * jnp.exp(-b_ref[s] * inverse)
        return carry

    lax.fori_loop(0, depth, rates, 0)
    local_pass(field, half, 0)

    if fused:
        load_n.wait()
        load_up.wait()
        load_e.wait()
        ranks_z = up_ref.shape[0]
        ranks_y = n_ref.shape[1]
        ranks_x = east.shape[1]
        own = ranks_y // ngz
        cells = depth * width
        for i, part in enumerate(split(east[...])):
            east_parts[i] = part
        rows, columns = up_parts.shape[1:]
        spread = dot(
            (iota((rows, ranks_z), 0) // width == iota((rows, ranks_z), 1)).astype(f32),
            up_ref[...],
        )
        heights = up_ref.shape[1]
        spread = dot(
            spread,
            (iota((heights, columns), 0) == iota((heights, columns), 1) // width).astype(f32),
        )
        spread = jnp.where(
            iota((rows, columns), 0) % width == iota((rows, columns), 1) % width, spread, 0.0
        )
        for i, part in enumerate(split(spread)):
            up_parts[i] = part
        rows, columns = north_parts.shape[1:]
        line = iota((rows, ranks_y), 0)
        pick = (line // (chunk_ranks * own)) * own + line % own == iota((rows, ranks_y), 1)
        spread = dot(pick.astype(f32), n_ref[...], (((1,), (1,)), ((), ())))
        widths = n_ref.shape[0]
        line = iota((widths, columns), 1)
        pick = (line // (chunk_ranks * width)) * width + line % width == iota((widths, columns), 0)
        spread = dot(spread, pick.astype(f32))
        spread = jnp.where(
            (iota((rows, columns), 0) // own) % chunk_ranks == (iota((rows, columns), 1) // width) % chunk_ranks,
            spread,
            0.0,
        )
        for i, part in enumerate(split(spread)):
            north_parts[i] = part

    def relay(s):
        wait_halos(0, s)
        fix(half, 0, s)
        send_halos(1, (0, 1), s)
        pack_rows(half, 1, s)
        send_halos(1, (2, 3), s)

    each_species(relay)
    local_pass(half, result, 1)

    def first_copy(s):
        return pltpu.make_async_remote_copy(
            src_ref=first.at[s],
            dst_ref=gathered.at[gz],
            send_sem=first_send.at[s],
            recv_sem=first_recv.at[gz],
            device_id={"gz": s},
            device_id_type=MESH,
        )

    def first_arrival(source):
        return pltpu.make_async_remote_copy(
            src_ref=gathered.at[source],
            dst_ref=gathered.at[source],
            send_sem=first_send.at[source],
            recv_sem=first_recv.at[source],
            device_id={"gz": source},
            device_id_type=MESH,
        )

    def finish(s):
        wait_halos(1, s)
        fix(result, 1, s)
        if fused:
            product = dot3(split(result[s].reshape(cells, length)), (east_parts[0], east_parts[1]))

            @pl.when(s == gz)
            def _():
                gathered[gz] = product

            @pl.when(s != gz)
            def _():
                first[s] = product
                first_copy(s).start()

    store = pltpu.make_async_copy(result, next_hbm, load_sem.at[3])

    if fused:
        block = chunk_ranks * width
        out = chunk_ranks * own
        chunks = ranks_z // chunk_ranks

        def room(way, n):
            return gy + n < ngy if way else gy >= n

        def line_copy(way, d, chunk, held):
            origin = gy - held if way else gy + held
            part = second.at[origin, chunk * block : (chunk + 1) * block]
            return pltpu.make_async_remote_copy(
                src_ref=part,
                dst_ref=part,
                send_sem=second_send.at[way, d, chunk],
                recv_sem=second_recv.at[way, d, chunk],
                device_id={"gy": gy + d - held if way else gy + held - d},
                device_id_type=MESH,
            )

        def line_arrival(way, d, chunk):
            origin = gy - d if way else gy + d
            part = second.at[origin, chunk * block : (chunk + 1) * block]
            return pltpu.make_async_remote_copy(
                src_ref=part,
                dst_ref=part,
                send_sem=second_send.at[way, d, chunk],
                recv_sem=second_recv.at[way, d, chunk],
                device_id={"gy": other[3 - way]},
                device_id_type=MESH,
            )

        def each_own(chunk, act):
            for d in range(1, ngy):
                for way in range(2):
                    if d != 2:

                        @pl.when(room(way, d))
                        def _(way=way, d=d):
                            act(line_copy(way, d, chunk, 0))

        def each_relayed(way, chunk, act):
            @pl.when(jnp.logical_and(room(1 - way, 1), room(way, 1)))
            def _():
                act(line_copy(way, 2, chunk, 1))

        def start(copy):
            copy.start()

        def wait_send(copy):
            copy.wait_send()

        def third_copy(k, chunk):
            peer = lax.rem(gz + k, ngz)
            rows = slice(chunk * out, (chunk + 1) * out)
            return pltpu.make_async_remote_copy(
                src_ref=slabs.at[peer, rows],
                dst_ref=core_hbm.at[gz, rows],
                send_sem=third_send.at[k, chunk],
                recv_sem=third_recv.at[k, chunk],
                device_id={"gz": peer},
                device_id_type=MESH,
            )

        def contract():
            for k in range(1, ngz):
                first_arrival(lax.rem(gz + k, ngz)).wait_recv()
            slab = split(gathered[...].reshape(ngz * cells, ranks_x))
            for chunk in range(chunks):
                rows = slice(chunk * block, (chunk + 1) * block)
                second[gy, rows] = dot3((up_parts[0, rows], up_parts[1, rows]), slab)
                each_own(chunk, start)

        each_species(finish)
        store.start()
        contract()
        for d in range(1, ngy):
            for chunk in range(chunks):
                for way in range(2):

                    @pl.when(room(1 - way, d))
                    def _(way=way, d=d, chunk=chunk):
                        line_arrival(way, d, chunk).wait_recv()

                    if d == 1:
                        each_relayed(way, chunk, start)
                if d == ngy - 1:
                    terms = second[:, chunk * block : (chunk + 1) * block, :]
                    product = dot3(
                        (north_parts[0], north_parts[1]), split(terms.reshape(ngy * block, ranks_x))
                    )
                    slabs[:, chunk * out : (chunk + 1) * out, :] = product.reshape(ngz, out, ranks_x)
                    for k in range(1, ngz):
                        third_copy(k, chunk).start()
        keep = pltpu.make_async_copy(slabs.at[gz], core_hbm.at[gz], load_sem.at[4])
        keep.start()
        for chunk in range(chunks):
            for k in range(1, ngz):
                third_copy(k, chunk).wait_recv()
        keep.wait()
        for k in range(1, ngz):
            first_copy(lax.rem(gz + k, ngz)).wait_send()
            for chunk in range(chunks):
                third_copy(k, chunk).wait_send()
        for chunk in range(chunks):
            each_own(chunk, wait_send)
            for way in range(2):
                each_relayed(way, chunk, wait_send)
    else:
        each_species(finish)
        store.start()

    store.wait()

    def drain(s):
        for stage in range(2):
            for side in range(4):

                @pl.when(has[side])
                def _(stage=stage, side=side):
                    halo_copy(stage, side, s).wait_send()

    each_species(drain)


def deliver_kernel(a_in, b_in, a_out, b_out, sems):
    copies = [
        pltpu.make_async_copy(a_in, a_out, sems.at[0]),
        pltpu.make_async_copy(b_in, b_out, sems.at[1]),
    ]
    for copy in copies:
        copy.start()
    for copy in copies:
        copy.wait()


def deliver(a, b):
    return pl.pallas_call(
        deliver_kernel,
        out_shape=[jax.ShapeDtypeStruct(x.shape, x.dtype) for x in (a, b)],
        in_specs=[pl.BlockSpec(memory_space=pl.ANY)] * 2,
        out_specs=[pl.BlockSpec(memory_space=pltpu.HBM)] * 2,
        scratch_shapes=[pltpu.SemaphoreType.DMA((2,))],
        compiler_params=pltpu.CompilerParams(vmem_limit_bytes=1 << 20),
        name="deliver",
    )(a, b)


def local(ngz, ngy, *args):
    u, t, d, a, b, m, e, n, up = args
    species, depth, width, length = u.shape
    ranks_x, ranks_y, ranks_z = e.shape[1], n.shape[1], up.shape[1]
    fused = species == ngz and species % 2 == 0 and ranks_z % chunk_ranks == 0 and ranks_y % ngz == 0
    fused = fused and chunk_ranks * (ranks_y // ngz) % 8 == 0
    anywhere = pl.BlockSpec(memory_space=pl.ANY)
    apart = pl.BlockSpec(memory_space=pltpu.HBM)
    packs = 2 * depth // width
    outputs = [jax.ShapeDtypeStruct(u.shape, f32)]
    padded = (species, depth + 4, width, length)
    scratch = [
        pltpu.VMEM(padded, f32),
        pltpu.VMEM(padded, f32),
        pltpu.VMEM(u.shape, f32),
        pltpu.VMEM(u.shape, f32),
        pltpu.VMEM(t.shape, f32),
        pltpu.VMEM((2, 2, species, 2, width, length), f32),
        pltpu.VMEM((2, 2, species, packs, width, length), f32),
        pltpu.VMEM((2, 2, species, packs, width, length), f32),
        pltpu.SMEM(d.shape, f32),
        pltpu.SMEM(a.shape, f32),
        pltpu.SMEM(b.shape, f32),
        pltpu.SMEM(m.shape, f32),
        pltpu.SemaphoreType.DMA((11,)),
        pltpu.SemaphoreType.DMA((2, 4, species)),
        pltpu.SemaphoreType.DMA((2, 4, species)),
    ]
    if fused:
        own = ranks_y // ngz
        cells = depth * width
        outputs.append(jax.ShapeDtypeStruct((species, ranks_z * own, ranks_x), f32))
        scratch += [
            pltpu.VMEM((length, ranks_x), f32),
            pltpu.VMEM(n.shape, f32),
            pltpu.VMEM(up.shape[::-1], f32),
            pltpu.VMEM((species, cells, ranks_x), f32),
            pltpu.VMEM((ngz, cells, ranks_x), f32),
            pltpu.VMEM((ngy, ranks_z * width, ranks_x), f32),
            pltpu.VMEM((ngz, ranks_z * own, ranks_x), f32),
            pltpu.VMEM((2, length, ranks_x), jnp.bfloat16),
            pltpu.VMEM((2, ranks_z * width, ngz * cells), jnp.bfloat16),
            pltpu.VMEM((2, ngz * chunk_ranks * own, ngy * chunk_ranks * width), jnp.bfloat16),
            pltpu.SemaphoreType.DMA((ngz,)),
            pltpu.SemaphoreType.DMA((ngz,)),
            pltpu.SemaphoreType.DMA((2, ngy, ranks_z // chunk_ranks)),
            pltpu.SemaphoreType.DMA((2, ngy, ranks_z // chunk_ranks)),
            pltpu.SemaphoreType.DMA((ngz, ranks_z // chunk_ranks)),
            pltpu.SemaphoreType.DMA((ngz, ranks_z // chunk_ranks)),
        ]
    outs = pl.pallas_call(
        functools.partial(kernel, ngz, ngy, fused),
        out_shape=outputs,
        in_specs=[apart] * 9,
        out_specs=[anywhere] * len(outputs),
        scratch_shapes=scratch,
        compiler_params=pltpu.CompilerParams(
            collective_id=0, has_side_effects=True, vmem_limit_bytes=48 << 20
        ),
        name="heun_step",
    )(*[pltpu.with_memory_space_constraint(x, pltpu.HBM) for x in (u, t, d, a, b, m, e, n, up.T)])
    if fused:
        outs = deliver(*outs)
        return outs[0], outs[1].reshape(species, ranks_z, own, ranks_x)
    species_next = outs[0]
    projected = jnp.einsum("szyx,xr->szyr", species_next, e, precision=HIGHEST)
    rows = lax.dynamic_slice_in_dim(n, lax.axis_index("gy") * width, width, 0)
    projected = jnp.einsum("szyr,yq->szqr", projected, rows, precision=HIGHEST)
    partial = jnp.einsum(
        "szqr,zp->spqr",
        lax.all_to_all(projected, "gz", split_axis=2, concat_axis=1, tiled=True),
        up,
        precision=HIGHEST,
    )
    return species_next, lax.psum(partial, "gy")


def solution(mesh):
    return jax.shard_map(
        functools.partial(local, mesh.shape["gz"], mesh.shape["gy"]),
        mesh=mesh,
        in_specs=(
            P(None, "gz", "gy", None),
            P("gz", "gy", None),
            P(),
            P(),
            P(),
            P(),
            P(),
            P(),
            P(),
        ),
        out_specs=(P(None, "gz", "gy", None), P(None, None, "gz", None)),
        check_vma=False,
    )
```

```python
import functools

import jax
import jax.numpy as jnp
from jax import lax
from jax.experimental import pallas as pl
from jax.experimental.pallas import tpu as pltpu
from jax.sharding import PartitionSpec as P

time_step = 0.1
chunk_ranks = 8
chunks = 4
ahead = 3
behind = 2
most_groups = 4
MESH = pl.DeviceIdType.MESH
HIGHEST = lax.Precision.HIGHEST
f32 = jnp.float32


def iota(shape, dim):
    return lax.broadcasted_iota(jnp.int32, shape, dim)


def dot(a, b, dims=(((1,), (0,)), ((), ()))):
    return lax.dot_general(a, b, dims, precision=HIGHEST, preferred_element_type=f32)


def split(x):
    top = x.astype(jnp.bfloat16)
    return top, (x - top.astype(f32)).astype(jnp.bfloat16)


def dot3(a, b):
    (a1, a2), (b1, b2) = a, b
    small = jnp.dot(a1, b2, preferred_element_type=f32)
    small += jnp.dot(a2, b1, preferred_element_type=f32)
    return small + jnp.dot(a1, b1, preferred_element_type=f32)


def kernel(ngz, ngy, fused, *refs):
    (
        u_hbm,
        t_hbm,
        d_hbm,
        a_hbm,
        b_hbm,
        m_hbm,
        e_hbm,
        n_hbm,
        up_hbm,
        next_hbm,
    ) = refs[:10]
    rest = refs[10:]
    if fused:
        core_hbm, rest = rest[0], rest[1:]
    (
        field,
        half,
        rate,
        result,
        thermal,
        zhalo,
        yhalo,
        ysend,
        d_ref,
        a_ref,
        b_ref,
        m_ref,
        load_sem,
        field_sem,
        halo_send,
        halo_recv,
    ) = rest[:16]
    if fused:
        (
            east,
            n_ref,
            up_ref,
            first,
            gathered,
            second,
            slabs,
            east_parts,
            up_parts,
            north_parts,
            first_send,
            first_recv,
            second_send,
            second_recv,
            third_send,
            third_recv,
        ) = rest[16:]

    species, depth, width, length = u_hbm.shape
    gz = lax.axis_index("gz")
    gy = lax.axis_index("gy")
    groups = halo_recv.shape[2]
    has = [gz > 0, gz < ngz - 1, gy > 0, gy < ngy - 1]
    names = ["gz", "gz", "gy", "gy"]
    other = [gz - 1, gz + 1, gy - 1, gy + 1]

    barrier = pltpu.get_barrier_semaphore()
    if fused:
        for k in range(1, ngz):
            pl.semaphore_signal(
                barrier, inc=1, device_id={"gz": lax.rem(gz + k, ngz)}, device_id_type=MESH
            )
        for k in range(1, ngy):
            pl.semaphore_signal(
                barrier, inc=1, device_id={"gy": lax.rem(gy + k, ngy)}, device_id_type=MESH
            )
    partners = () if fused else (0, 1, 2, 3)
    for side in partners:

        @pl.when(has[side])
        def _(side=side):
            pl.semaphore_signal(
                barrier, inc=1, device_id={names[side]: other[side]}, device_id_type=MESH
            )

    load_t = pltpu.make_async_copy(t_hbm, thermal, load_sem.at[1])
    small = [
        pltpu.make_async_copy(src, dst, load_sem.at[5 + i])
        for i, (src, dst) in enumerate(
            ((d_hbm, d_ref), (a_hbm, a_ref), (b_hbm, b_ref), (m_hbm, m_ref))
        )
    ]
    load_u = [
        pltpu.make_async_copy(
            u_hbm.at[lo : lo + species // groups],
            field.at[lo : lo + species // groups, 2 : 2 + depth],
            field_sem.at[group],
        )
        for group in range(groups)
        for lo in [group * (species // groups)]
    ]
    for copy in load_u:
        copy.start()
    for copy in small:
        copy.start()
    load_t.start()
    if fused:
        load_e = pltpu.make_async_copy(e_hbm, east, load_sem.at[2])
        load_n = pltpu.make_async_copy(n_hbm, n_ref, load_sem.at[9])
        load_up = pltpu.make_async_copy(up_hbm, up_ref, load_sem.at[4])
        for copy in (load_e, load_n, load_up):
            copy.start()

    row = iota((width, length), 0)
    lane = iota((width, length), 1)
    per = width // 2
    packs = depth // per

    def weight(s, stage):
        return d_ref[s] * (time_step / 12.0 * (0.5 if stage else 1.0))

    members = species // groups

    def each_member(group, step):
        def body(s, carry):
            step(s)
            return carry

        lax.fori_loop(group * members, (group + 1) * members, body, 0)

    def span(group):
        return slice(group * members, (group + 1) * members)

    def pack_rows(source, stage, s):
        first_gain = jnp.where(row == 0, 16.0, 0.0)
        last_gain = jnp.where(row == width - 1, 16.0, 0.0)

        k = weight(s, stage)
        for group in range(packs):
            up = jnp.zeros((width, length), f32)
            down = jnp.zeros((width, length), f32)
            for i in range(per):
                v = source[s, 2 + group * per + i] * k
                rising = first_gain * pltpu.roll(v, 1, 0) - pltpu.roll(v, 2, 0)
                falling = last_gain * pltpu.roll(v, width - 1, 0) - pltpu.roll(
                    v, width - 2, 0
                )
                here = jnp.logical_and(row >= 2 * i, row < 2 * i + 2)
                if i:
                    rising = pltpu.roll(rising, 2 * i, 0)
                falling = pltpu.roll(falling, (2 * i + 2) % width, 0) if i < per - 1 else falling
                up = jnp.where(here, rising, up)
                down = jnp.where(here, falling, down)
            ysend[stage, 0, s, group] = down
            ysend[stage, 1, s, group] = up

    def halo_copy(stage, side, group):
        who = span(group)
        if side < 2:
            start = 0 if side == 0 else depth - 2
            if stage == 0:
                src = u_hbm.at[who, start : start + 2]
            else:
                src = half.at[who, 2 + start : 4 + start]
            dst = zhalo.at[stage, 1 - side, who]
        else:
            src = ysend.at[stage, side - 2, who]
            dst = yhalo.at[stage, 3 - side, who]
        opposite = side ^ 1
        return pltpu.make_async_remote_copy(
            src_ref=src,
            dst_ref=dst,
            send_sem=halo_send.at[stage, side, group],
            recv_sem=halo_recv.at[stage, opposite, group],
            device_id={names[side]: other[side]},
            device_id_type=MESH,
        )

    def arrived(stage, side, group):
        who = span(group)
        dst = zhalo.at[stage, side, who] if side < 2 else yhalo.at[stage, side - 2, who]
        return pltpu.make_async_remote_copy(
            src_ref=dst,
            dst_ref=dst,
            send_sem=halo_send.at[stage, side, group],
            recv_sem=halo_recv.at[stage, side, group],
            device_id={names[side]: other[side]},
            device_id_type=MESH,
        )

    def send_halos(stage, sides, group):
        for side in sides:

            @pl.when(has[side])
            def _(side=side):
                halo_copy(stage, side, group).start()

    def wait_halos(stage, group):
        for side in range(4):

            @pl.when(has[side])
            def _(side=side):
                arrived(stage, side, group).wait_recv()

    def drain(stage, group):
        for side in range(4):

            @pl.when(has[side])
            def _(side=side):
                halo_copy(stage, side, group).wait_send()

    def local_pass(source, target, stage):
        offset = 0 if stage else 2
        gain = 0.5 if stage else 1.0

        def body(z, carry):
            for s in range(species):
                c = source[s, z + 2]
                near = source[s, z + 1] + source[s, z + 3]
                far = source[s, z] + source[s, z + 4]
                near += jnp.where(row >= 1, pltpu.roll(c, 1, 0), 0.0)
                near += jnp.where(row < width - 1, pltpu.roll(c, width - 1, 0), 0.0)
                far += jnp.where(row >= 2, pltpu.roll(c, 2, 0), 0.0)
                far += jnp.where(row < width - 2, pltpu.roll(c, width - 2, 0), 0.0)
                near += jnp.where(lane >= 1, pltpu.roll(c, 1, 1), 0.0)
                near += jnp.where(lane < length - 1, pltpu.roll(c, length - 1, 1), 0.0)
                far += jnp.where(lane >= 2, pltpu.roll(c, 2, 1), 0.0)
                far += jnp.where(lane < length - 2, pltpu.roll(c, length - 2, 1), 0.0)
                total = weight(s, stage) * (16.0 * near - far - 90.0 * c)
                if stage:
                    total += 0.5 * (c + field[s, z + 2])
                else:
                    total += c
                target[s, z + offset] = total
            for tile in range(0, length, 128):
                part = pl.ds(tile, 128)
                turnover = [
                    (rate[t, z, :, part] * source[t, z + 2, :, part]) * (gain * time_step)
                    for t in range(species)
                ]
                for s in range(species):
                    total = target[s, z + offset, :, part] - turnover[s]
                    for t in range(species):
                        total += m_ref[s, t] * turnover[t]
                    target[s, z + offset, :, part] = total
            return carry

        lax.fori_loop(0, depth, body, 0)

    def fix(target, stage, s):
        offset = 0 if stage else 2

        k = weight(s, stage)
        add = {}
        below, above = zhalo[stage, 0, s], zhalo[stage, 1, s]
        add[0] = k * (16.0 * below[1] - below[0])
        add[1] = -k * below[1]
        add[depth - 1] = k * (16.0 * above[0] - above[1])
        add[depth - 2] = -k * above[0]
        for group in range(packs):
            low, high = yhalo[stage, 0, s, group], yhalo[stage, 1, s, group]
            for i in range(per):
                z = group * per + i
                shift = (width - 2 * i) % width
                value = target[s, z + offset]
                value += jnp.where(row < 2, pltpu.roll(low, shift, 0) if shift else low, 0.0)
                shift = (2 * width - 2 - 2 * i) % width
                value += jnp.where(
                    row >= width - 2, pltpu.roll(high, shift, 0) if shift else high, 0.0
                )
                if z in add:
                    value += add[z]
                target[s, z + offset] = value

    if fused:
        pl.semaphore_wait(barrier, ngz + ngy - 2)
    for side in partners:

        @pl.when(has[side])
        def _():
            pl.semaphore_wait(barrier, 1)

    for group in range(groups):
        send_halos(0, (0, 1), group)
    for copy in small:
        copy.wait()
    for group in range(groups):
        load_u[group].wait()
        each_member(group, lambda s: pack_rows(field, 0, s))
        send_halos(0, (2, 3), group)

    zeros = jnp.zeros((species, 2, width, length), f32)
    for buffer in (field, half):
        buffer[:, 0:2] = zeros
        buffer[:, 2 + depth : 4 + depth] = zeros
    for side in range(2):

        @pl.when(jnp.logical_not(has[side]))
        def _(side=side):
            for stage in range(2):
                zhalo[stage, side] = zeros

        @pl.when(jnp.logical_not(has[2 + side]))
        def _(side=side):
            for stage in range(2):
                yhalo[stage, side] = jnp.zeros(yhalo.shape[2:], f32)

    load_t.wait()

    def rates(z, carry):
        inverse = 1.0 / thermal[z]
        for s in range(species):
            rate[s, z] = a_ref[s] * jnp.exp(-b_ref[s] * inverse)
        return carry

    lax.fori_loop(0, depth, rates, 0)
    local_pass(field, half, 0)

    if fused:
        load_n.wait()
        load_up.wait()
        load_e.wait()
        ranks_z = up_ref.shape[0]
        ranks_y = n_ref.shape[1]
        ranks_x = east.shape[1]
        own = ranks_y // ngz
        cells = depth * width
        for i, part in enumerate(split(east[...])):
            east_parts[i] = part
        rows, columns = up_parts.shape[1:]
        spread = dot(
            (iota((rows, ranks_z), 0) // width == iota((rows, ranks_z), 1)).astype(f32),
            up_ref[...],
        )
        heights = up_ref.shape[1]
        spread = dot(
            spread,
            (iota((heights, columns), 0) == iota((heights, columns), 1) // width).astype(f32),
        )
        spread = jnp.where(
            iota((rows, columns), 0) % width == iota((rows, columns), 1) % width, spread, 0.0
        )
        for i, part in enumerate(split(spread)):
            up_parts[i] = part
        rows, columns = north_parts.shape[1:]
        line = iota((rows, ranks_y), 0)
        pick = (line // (chunk_ranks * own)) * own + line % own == iota((rows, ranks_y), 1)
        spread = dot(pick.astype(f32), n_ref[...], (((1,), (1,)), ((), ())))
        widths = n_ref.shape[0]
        line = iota((widths, columns), 1)
        pick = (line // (chunk_ranks * width)) * width + line % width == iota((widths, columns), 0)
        spread = dot(spread, pick.astype(f32))
        spread = jnp.where(
            (iota((rows, columns), 0) // own) % chunk_ranks == (iota((rows, columns), 1) // width) % chunk_ranks,
            spread,
            0.0,
        )
        for i, part in enumerate(split(spread)):
            north_parts[i] = part

    for group in range(groups):
        wait_halos(0, group)

        def relay(s):
            fix(half, 0, s)
            pack_rows(half, 1, s)

        each_member(group, relay)
        send_halos(1, (2, 3, 0, 1), group)
    local_pass(half, result, 1)

    def owner(s):
        return s * 2 % species + s * 2 // species

    def first_copy(s):
        return pltpu.make_async_remote_copy(
            src_ref=first.at[s],
            dst_ref=gathered.at[gz],
            send_sem=first_send.at[0],
            recv_sem=first_recv.at[0],
            device_id={"gz": owner(s)},
            device_id_type=MESH,
        )

    def first_all():
        part = gathered.at[0 : ngz - 1]
        return pltpu.make_async_remote_copy(
            src_ref=part,
            dst_ref=part,
            send_sem=first_send.at[0],
            recv_sem=first_recv.at[0],
            device_id={"gz": lax.rem(gz + 1, ngz)},
            device_id_type=MESH,
        )

    def project(group):
        rows = result[span(group)].reshape(members * cells, length)
        product = dot3(split(rows), (east_parts[0], east_parts[1]))
        for i in range(members):
            s = group * members + i
            part = product[i * cells : (i + 1) * cells]

            @pl.when(gz == owner(s))
            def _(s=s, part=part):
                gathered[owner(s)] = part

            @pl.when(gz != owner(s))
            def _(s=s, part=part):
                first[s] = part
                first_copy(s).start()

    store = pltpu.make_async_copy(result, next_hbm, load_sem.at[3])

    if fused:
        piece = chunk_ranks * width
        few = chunk_ranks * own
        parts = ranks_z // chunk_ranks // chunks
        block = parts * piece
        out = parts * few

        mine = gz // 2 + lax.rem(gz, 2) * (species // 2)

        def room(way, n):
            return gy + n < ngy if way else gy >= n

        def line_copy(way, d, chunk, held):
            origin = gy - held if way else gy + held
            part = second.at[origin, chunk * block : (chunk + 1) * block]
            return pltpu.make_async_remote_copy(
                src_ref=part,
                dst_ref=part,
                send_sem=second_send.at[way, d - 1, chunk],
                recv_sem=second_recv.at[way, d - 1, chunk],
                device_id={"gy": gy + d - held if way else gy + held - d},
                device_id_type=MESH,
            )

        def line_arrival(way, d, chunk):
            origin = gy - d if way else gy + d
            part = second.at[origin, chunk * block : (chunk + 1) * block]
            return pltpu.make_async_remote_copy(
                src_ref=part,
                dst_ref=part,
                send_sem=second_send.at[way, d - 1, chunk],
                recv_sem=second_recv.at[way, d - 1, chunk],
                device_id={"gy": other[3 - way]},
                device_id_type=MESH,
            )

        def each_own(chunk, act):
            for d in range(1, ngy):
                for way in range(2):
                    if d != 2:

                        @pl.when(room(way, d))
                        def _(way=way, d=d):
                            act(line_copy(way, d, chunk, 0))

        def each_relayed(way, chunk, act):
            @pl.when(jnp.logical_and(room(1 - way, 1), room(way, 1)))
            def _():
                act(line_copy(way, 2, chunk, 1))

        def start(copy):
            copy.start()

        def wait_send(copy):
            copy.wait_send()

        def third_copy(k, chunk):
            peer = lax.rem(gz + k, ngz)
            rows = slice(chunk * out, (chunk + 1) * out)
            return pltpu.make_async_remote_copy(
                src_ref=slabs.at[peer, rows],
                dst_ref=core_hbm.at[mine, rows],
                send_sem=third_send.at[chunk],
                recv_sem=third_recv.at[chunk],
                device_id={"gz": peer},
                device_id_type=MESH,
            )

        def third_all(chunk):
            rows = slice(chunk * out, (chunk + 1) * out)
            return pltpu.make_async_remote_copy(
                src_ref=slabs.at[0 : ngz - 1, rows],
                dst_ref=core_hbm.at[0 : ngz - 1, rows],
                send_sem=third_send.at[chunk],
                recv_sem=third_recv.at[chunk],
                device_id={"gz": lax.rem(gz + 1, ngz)},
                device_id_type=MESH,
            )

        def contract():
            first_all().wait_recv()
            slab = split(gathered[...].reshape(ngz * cells, ranks_x))
            second[gy] = dot3((up_parts[0], up_parts[1]), slab)

        for group in range(groups):
            wait_halos(1, group)
            each_member(group, lambda s: fix(result, 1, s))
            project(group)
        store.start()
        contract()
        def await_line(d, chunk):
            for way in range(2):

                @pl.when(room(1 - way, d))
                def _(way=way):
                    line_arrival(way, d, chunk).wait_recv()

        def open_line(chunk):
            await_line(1, chunk)
            for way in range(2):
                each_relayed(way, chunk, start)

        def finish(chunk):
            for d in range(2, ngy):
                await_line(d, chunk)
            for part in range(parts):
                lines = slice(chunk * block + part * piece, chunk * block + (part + 1) * piece)
                rows = slice(chunk * out + part * few, chunk * out + (part + 1) * few)
                terms = second[:, lines, :].reshape(ngy * piece, ranks_x)
                product = dot3((north_parts[0], north_parts[1]), split(terms))
                slabs[:, rows, :] = product.reshape(ngz, few, ranks_x)
            for k in range(1, ngz):
                third_copy(k, chunk).start()

        for chunk in range(min(ahead, chunks)):
            each_own(chunk, start)
        for chunk in range(chunks):
            open_line(chunk)
            if chunk + ahead < chunks:
                each_own(chunk + ahead, start)
            if chunk >= behind:
                finish(chunk - behind)
        for chunk in range(chunks - behind, chunks):
            finish(chunk)
        keep = pltpu.make_async_copy(slabs.at[gz], core_hbm.at[mine], load_sem.at[0])
        keep.start()
        for chunk in range(chunks):
            third_all(chunk).wait_recv()
        keep.wait()
        first_all().wait_send()
        for chunk in range(chunks):
            third_all(chunk).wait_send()
        for chunk in range(chunks):
            each_own(chunk, wait_send)
            for way in range(2):
                each_relayed(way, chunk, wait_send)
    else:
        for group in range(groups):
            wait_halos(1, group)
            each_member(group, lambda s: fix(result, 1, s))
        store.start()

    store.wait()

    for stage in range(2):
        for group in range(groups):
            drain(stage, group)


def deliver_kernel(a_in, b_in, a_out, b_out, sems):
    copies = [
        pltpu.make_async_copy(a_in, a_out, sems.at[0]),
        pltpu.make_async_copy(b_in, b_out, sems.at[1]),
    ]
    for copy in copies:
        copy.start()
    for copy in copies:
        copy.wait()


def deliver(a, b):
    return pl.pallas_call(
        deliver_kernel,
        out_shape=[jax.ShapeDtypeStruct(x.shape, x.dtype) for x in (a, b)],
        in_specs=[pl.BlockSpec(memory_space=pl.ANY)] * 2,
        out_specs=[pl.BlockSpec(memory_space=pltpu.HBM)] * 2,
        scratch_shapes=[pltpu.SemaphoreType.DMA((2,))],
        compiler_params=pltpu.CompilerParams(vmem_limit_bytes=1 << 20),
        name="deliver",
    )(a, b)


def local(ngz, ngy, *args):
    u, t, d, a, b, m, e, n, up = args
    species, depth, width, length = u.shape
    ranks_x, ranks_y, ranks_z = e.shape[1], n.shape[1], up.shape[1]
    fused = species == ngz and species % 2 == 0 and ranks_z % (chunk_ranks * chunks) == 0 and ranks_y % ngz == 0
    fused = fused and chunk_ranks * (ranks_y // ngz) % 8 == 0
    anywhere = pl.BlockSpec(memory_space=pl.ANY)
    apart = pl.BlockSpec(memory_space=pltpu.HBM)
    packs = 2 * depth // width
    groups = most_groups if species % most_groups == 0 else 1
    outputs = [jax.ShapeDtypeStruct(u.shape, f32)]
    padded = (species, depth + 4, width, length)
    scratch = [
        pltpu.VMEM(padded, f32),
        pltpu.VMEM(padded, f32),
        pltpu.VMEM(u.shape, f32),
        pltpu.VMEM(u.shape, f32),
        pltpu.VMEM(t.shape, f32),
        pltpu.VMEM((2, 2, species, 2, width, length), f32),
        pltpu.VMEM((2, 2, species, packs, width, length), f32),
        pltpu.VMEM((2, 2, species, packs, width, length), f32),
        pltpu.SMEM(d.shape, f32),
        pltpu.SMEM(a.shape, f32),
        pltpu.SMEM(b.shape, f32),
        pltpu.SMEM(m.shape, f32),
        pltpu.SemaphoreType.DMA((10,)),
        pltpu.SemaphoreType.DMA((groups,)),
        pltpu.SemaphoreType.DMA((2, 4, groups)),
        pltpu.SemaphoreType.DMA((2, 4, groups)),
    ]
    if fused:
        own = ranks_y // ngz
        cells = depth * width
        outputs.append(jax.ShapeDtypeStruct((species, ranks_z * own, ranks_x), f32))
        scratch += [
            pltpu.VMEM((length, ranks_x), f32),
            pltpu.VMEM(n.shape, f32),
            pltpu.VMEM(up.shape[::-1], f32),
            pltpu.VMEM((species, cells, ranks_x), f32),
            pltpu.VMEM((ngz, cells, ranks_x), f32),
            pltpu.VMEM((ngy, ranks_z * width, ranks_x), f32),
            pltpu.VMEM((ngz, ranks_z * own, ranks_x), f32),
            pltpu.VMEM((2, length, ranks_x), jnp.bfloat16),
            pltpu.VMEM((2, ranks_z * width, ngz * cells), jnp.bfloat16),
            pltpu.VMEM((2, ngz * chunk_ranks * own, ngy * chunk_ranks * width), jnp.bfloat16),
            pltpu.SemaphoreType.DMA((1,)),
            pltpu.SemaphoreType.DMA((1,)),
            pltpu.SemaphoreType.DMA((2, ngy - 1, chunks)),
            pltpu.SemaphoreType.DMA((2, ngy - 1, chunks)),
            pltpu.SemaphoreType.DMA((chunks,)),
            pltpu.SemaphoreType.DMA((chunks,)),
        ]
    outs = pl.pallas_call(
        functools.partial(kernel, ngz, ngy, fused),
        out_shape=outputs,
        in_specs=[apart] * 9,
        out_specs=[anywhere] * len(outputs),
        scratch_shapes=scratch,
        compiler_params=pltpu.CompilerParams(
            collective_id=0, has_side_effects=True, vmem_limit_bytes=48 << 20
        ),
        name="heun_step",
    )(*[pltpu.with_memory_space_constraint(x, pltpu.HBM) for x in (u, t, d, a, b, m, e, n, up.T)])
    if fused:
        outs = deliver(*outs)
        return outs[0], outs[1].reshape(species, ranks_z, own, ranks_x)
    species_next = outs[0]
    projected = jnp.einsum("szyx,xr->szyr", species_next, e, precision=HIGHEST)
    rows = lax.dynamic_slice_in_dim(n, lax.axis_index("gy") * width, width, 0)
    projected = jnp.einsum("szyr,yq->szqr", projected, rows, precision=HIGHEST)
    partial = jnp.einsum(
        "szqr,zp->spqr",
        lax.all_to_all(projected, "gz", split_axis=2, concat_axis=1, tiled=True),
        up,
        precision=HIGHEST,
    )
    return species_next, lax.psum(partial, "gy")


def solution(mesh):
    return jax.shard_map(
        functools.partial(local, mesh.shape["gz"], mesh.shape["gy"]),
        mesh=mesh,
        in_specs=(
            P(None, "gz", "gy", None),
            P("gz", "gy", None),
            P(),
            P(),
            P(),
            P(),
            P(),
            P(),
            P(),
        ),
        out_specs=(P(None, "gz", "gy", None), P(None, None, "gz", None)),
        check_vma=False,
    )
```

```python
import functools

import jax
import jax.numpy as jnp
from jax import lax
from jax.experimental import pallas as pl
from jax.experimental.pallas import tpu as pltpu
from jax.sharding import PartitionSpec as P

time_step = 0.1
chunk_ranks = 8
chunks = 4
ahead = 3
behind = 2
most_groups = 4
MESH = pl.DeviceIdType.MESH
HIGHEST = lax.Precision.HIGHEST
f32 = jnp.float32


def iota(shape, dim):
    return lax.broadcasted_iota(jnp.int32, shape, dim)


def dot(a, b, dims=(((1,), (0,)), ((), ()))):
    return lax.dot_general(a, b, dims, precision=HIGHEST, preferred_element_type=f32)


def split(x):
    top = x.astype(jnp.bfloat16)
    return top, (x - top.astype(f32)).astype(jnp.bfloat16)


def dot3(a, b):
    (a1, a2), (b1, b2) = a, b
    small = jnp.dot(a1, b2, preferred_element_type=f32)
    small += jnp.dot(a2, b1, preferred_element_type=f32)
    return small + jnp.dot(a1, b1, preferred_element_type=f32)


def kernel(ngz, ngy, fused, *refs):
    (
        u_hbm,
        t_hbm,
        d_hbm,
        a_hbm,
        b_hbm,
        m_hbm,
        e_hbm,
        n_hbm,
        up_hbm,
        next_hbm,
    ) = refs[:10]
    rest = refs[10:]
    if fused:
        core_hbm, rest = rest[0], rest[1:]
    (
        field,
        half,
        rate,
        result,
        thermal,
        zhalo,
        yhalo,
        ysend,
        d_ref,
        a_ref,
        b_ref,
        m_ref,
        load_sem,
        field_sem,
        halo_send,
        halo_recv,
    ) = rest[:16]
    if fused:
        (
            east,
            n_ref,
            up_ref,
            first,
            gathered,
            second,
            slabs,
            east_parts,
            up_parts,
            north_parts,
            first_send,
            first_recv,
            second_send,
            second_recv,
            third_send,
            third_recv,
        ) = rest[16:]

    species, depth, width, length = u_hbm.shape
    gz = lax.axis_index("gz")
    gy = lax.axis_index("gy")
    groups = halo_recv.shape[2]
    has = [gz > 0, gz < ngz - 1, gy > 0, gy < ngy - 1]
    names = ["gz", "gz", "gy", "gy"]
    other = [gz - 1, gz + 1, gy - 1, gy + 1]

    barrier = pltpu.get_barrier_semaphore()
    if fused:
        for k in range(1, ngz):
            pl.semaphore_signal(
                barrier, inc=1, device_id={"gz": lax.rem(gz + k, ngz)}, device_id_type=MESH
            )
        for k in range(1, ngy):
            pl.semaphore_signal(
                barrier, inc=1, device_id={"gy": lax.rem(gy + k, ngy)}, device_id_type=MESH
            )
    partners = () if fused else (0, 1, 2, 3)
    for side in partners:

        @pl.when(has[side])
        def _(side=side):
            pl.semaphore_signal(
                barrier, inc=1, device_id={names[side]: other[side]}, device_id_type=MESH
            )

    load_t = pltpu.make_async_copy(t_hbm, thermal, load_sem.at[1])
    small = [
        pltpu.make_async_copy(src, dst, load_sem.at[5 + i])
        for i, (src, dst) in enumerate(
            ((d_hbm, d_ref), (a_hbm, a_ref), (b_hbm, b_ref), (m_hbm, m_ref))
        )
    ]
    load_u = [
        pltpu.make_async_copy(
            u_hbm.at[lo : lo + species // groups],
            field.at[lo : lo + species // groups, 2 : 2 + depth],
            field_sem.at[group],
        )
        for group in range(groups)
        for lo in [group * (species // groups)]
    ]
    for copy in load_u:
        copy.start()
    for copy in small:
        copy.start()
    load_t.start()
    if fused:
        load_e = pltpu.make_async_copy(e_hbm, east, load_sem.at[2])
        load_n = pltpu.make_async_copy(n_hbm, n_ref, load_sem.at[9])
        load_up = pltpu.make_async_copy(up_hbm, up_ref, load_sem.at[4])
        for copy in (load_e, load_n, load_up):
            copy.start()

    row = iota((width, length), 0)
    lane = iota((width, length), 1)
    per = width // 2
    packs = depth // per

    def weight(s, stage):
        return d_ref[s] * (time_step / 12.0 * (0.5 if stage else 1.0))

    members = species // groups

    def each_member(group, step):
        def body(s, carry):
            step(s)
            return carry

        lax.fori_loop(group * members, (group + 1) * members, body, 0)

    def span(group):
        return slice(group * members, (group + 1) * members)

    def pack_rows(source, stage, s):
        first_gain = jnp.where(row == 0, 16.0, 0.0)
        last_gain = jnp.where(row == width - 1, 16.0, 0.0)

        k = weight(s, stage)
        for group in range(packs):
            up = jnp.zeros((width, length), f32)
            down = jnp.zeros((width, length), f32)
            for i in range(per):
                v = source[s, 2 + group * per + i] * k
                rising = first_gain * pltpu.roll(v, 1, 0) - pltpu.roll(v, 2, 0)
                falling = last_gain * pltpu.roll(v, width - 1, 0) - pltpu.roll(
                    v, width - 2, 0
                )
                here = jnp.logical_and(row >= 2 * i, row < 2 * i + 2)
                if i:
                    rising = pltpu.roll(rising, 2 * i, 0)
                falling = pltpu.roll(falling, (2 * i + 2) % width, 0) if i < per - 1 else falling
                up = jnp.where(here, rising, up)
                down = jnp.where(here, falling, down)
            ysend[stage, 0, s, group] = down
            ysend[stage, 1, s, group] = up

    def halo_copy(stage, side, group):
        who = span(group)
        if side < 2:
            start = 0 if side == 0 else depth - 2
            if stage == 0:
                src = u_hbm.at[who, start : start + 2]
            else:
                src = half.at[who, 2 + start : 4 + start]
            dst = zhalo.at[stage, 1 - side, who]
        else:
            src = ysend.at[stage, side - 2, who]
            dst = yhalo.at[stage, 3 - side, who]
        opposite = side ^ 1
        return pltpu.make_async_remote_copy(
            src_ref=src,
            dst_ref=dst,
            send_sem=halo_send.at[stage, side],
            recv_sem=halo_recv.at[stage, opposite, group],
            device_id={names[side]: other[side]},
            device_id_type=MESH,
        )

    def arrived(stage, side, group):
        who = span(group)
        dst = zhalo.at[stage, side, who] if side < 2 else yhalo.at[stage, side - 2, who]
        return pltpu.make_async_remote_copy(
            src_ref=dst,
            dst_ref=dst,
            send_sem=halo_send.at[stage, side],
            recv_sem=halo_recv.at[stage, side, group],
            device_id={names[side]: other[side]},
            device_id_type=MESH,
        )

    def send_halos(stage, sides, group):
        for side in sides:

            @pl.when(has[side])
            def _(side=side):
                halo_copy(stage, side, group).start()

    def wait_halos(stage, group):
        for side in range(4):

            @pl.when(has[side])
            def _(side=side):
                arrived(stage, side, group).wait_recv()

    def drain():
        for stage in range(2):
            for side in range(4):

                @pl.when(has[side])
                def _(stage=stage, side=side):
                    sent = zhalo.at[stage, side] if side < 2 else ysend.at[stage, side - 2]
                    pltpu.make_async_remote_copy(
                        src_ref=sent,
                        dst_ref=sent,
                        send_sem=halo_send.at[stage, side],
                        recv_sem=halo_recv.at[stage, side, 0],
                        device_id={names[side]: other[side]},
                        device_id_type=MESH,
                    ).wait_send()

    def local_pass(source, target, stage):
        offset = 0 if stage else 2
        gain = 0.5 if stage else 1.0

        def body(z, carry):
            for s in range(species):
                c = source[s, z + 2]
                near = source[s, z + 1] + source[s, z + 3]
                far = source[s, z] + source[s, z + 4]
                near += jnp.where(row >= 1, pltpu.roll(c, 1, 0), 0.0)
                near += jnp.where(row < width - 1, pltpu.roll(c, width - 1, 0), 0.0)
                far += jnp.where(row >= 2, pltpu.roll(c, 2, 0), 0.0)
                far += jnp.where(row < width - 2, pltpu.roll(c, width - 2, 0), 0.0)
                near += jnp.where(lane >= 1, pltpu.roll(c, 1, 1), 0.0)
                near += jnp.where(lane < length - 1, pltpu.roll(c, length - 1, 1), 0.0)
                far += jnp.where(lane >= 2, pltpu.roll(c, 2, 1), 0.0)
                far += jnp.where(lane < length - 2, pltpu.roll(c, length - 2, 1), 0.0)
                total = weight(s, stage) * (16.0 * near - far - 90.0 * c)
                if stage:
                    total += 0.5 * (c + field[s, z + 2])
                else:
                    total += c
                target[s, z + offset] = total
            for tile in range(0, length, 128):
                part = pl.ds(tile, 128)
                turnover = [
                    (rate[t, z, :, part] * source[t, z + 2, :, part]) * (gain * time_step)
                    for t in range(species)
                ]
                for s in range(species):
                    total = target[s, z + offset, :, part] - turnover[s]
                    for t in range(species):
                        total += m_ref[s, t] * turnover[t]
                    target[s, z + offset, :, part] = total
            return carry

        lax.fori_loop(0, depth, body, 0)

    def fix(target, stage, s):
        offset = 0 if stage else 2

        k = weight(s, stage)
        add = {}
        below, above = zhalo[stage, 0, s], zhalo[stage, 1, s]
        add[0] = k * (16.0 * below[1] - below[0])
        add[1] = -k * below[1]
        add[depth - 1] = k * (16.0 * above[0] - above[1])
        add[depth - 2] = -k * above[0]
        for group in range(packs):
            low, high = yhalo[stage, 0, s, group], yhalo[stage, 1, s, group]
            for i in range(per):
                z = group * per + i
                shift = (width - 2 * i) % width
                value = target[s, z + offset]
                value += jnp.where(row < 2, pltpu.roll(low, shift, 0) if shift else low, 0.0)
                shift = (2 * width - 2 - 2 * i) % width
                value += jnp.where(
                    row >= width - 2, pltpu.roll(high, shift, 0) if shift else high, 0.0
                )
                if z in add:
                    value += add[z]
                target[s, z + offset] = value

    if fused:
        pl.semaphore_wait(barrier, ngz + ngy - 2)
    for side in partners:

        @pl.when(has[side])
        def _():
            pl.semaphore_wait(barrier, 1)

    for group in range(groups):
        send_halos(0, (0, 1), group)
    for copy in small:
        copy.wait()
    for group in range(groups):
        load_u[group].wait()
        each_member(group, lambda s: pack_rows(field, 0, s))
        send_halos(0, (2, 3), group)

    zeros = jnp.zeros((species, 2, width, length), f32)
    for buffer in (field, half):
        buffer[:, 0:2] = zeros
        buffer[:, 2 + depth : 4 + depth] = zeros
    for side in range(2):

        @pl.when(jnp.logical_not(has[side]))
        def _(side=side):
            for stage in range(2):
                zhalo[stage, side] = zeros

        @pl.when(jnp.logical_not(has[2 + side]))
        def _(side=side):
            for stage in range(2):
                yhalo[stage, side] = jnp.zeros(yhalo.shape[2:], f32)

    load_t.wait()

    def rates(z, carry):
        inverse = 1.0 / thermal[z]
        for s in range(species):
            rate[s, z] = a_ref[s] * jnp.exp(-b_ref[s] * inverse)
        return carry

    lax.fori_loop(0, depth, rates, 0)
    local_pass(field, half, 0)

    if fused:
        load_n.wait()
        load_up.wait()
        load_e.wait()
        ranks_z = up_ref.shape[0]
        ranks_y = n_ref.shape[1]
        ranks_x = east.shape[1]
        own = ranks_y // ngz
        cells = depth * width
        for i, part in enumerate(split(east[...])):
            east_parts[i] = part
        rows, columns = up_parts.shape[1:]
        spread = dot(
            (iota((rows, ranks_z), 0) // width == iota((rows, ranks_z), 1)).astype(f32),
            up_ref[...],
        )
        heights = up_ref.shape[1]
        spread = dot(
            spread,
            (iota((heights, columns), 0) == iota((heights, columns), 1) // width).astype(f32),
        )
        spread = jnp.where(
            iota((rows, columns), 0) % width == iota((rows, columns), 1) % width, spread, 0.0
        )
        for i, part in enumerate(split(spread)):
            up_parts[i] = part
        rows, columns = north_parts.shape[1:]
        line = iota((rows, ranks_y), 0)
        pick = (line // (chunk_ranks * own)) * own + line % own == iota((rows, ranks_y), 1)
        spread = dot(pick.astype(f32), n_ref[...], (((1,), (1,)), ((), ())))
        widths = n_ref.shape[0]
        line = iota((widths, columns), 1)
        pick = (line // (chunk_ranks * width)) * width + line % width == iota((widths, columns), 0)
        spread = dot(spread, pick.astype(f32))
        spread = jnp.where(
            (iota((rows, columns), 0) // own) % chunk_ranks == (iota((rows, columns), 1) // width) % chunk_ranks,
            spread,
            0.0,
        )
        for i, part in enumerate(split(spread)):
            north_parts[i] = part

    for group in range(groups):
        wait_halos(0, group)

        def relay(s):
            fix(half, 0, s)
            pack_rows(half, 1, s)

        each_member(group, relay)
        send_halos(1, (2, 3, 0, 1), group)
    local_pass(half, result, 1)

    def owner(s):
        return s * 2 % species + s * 2 // species

    def first_copy(s):
        return pltpu.make_async_remote_copy(
            src_ref=first.at[s],
            dst_ref=gathered.at[gz],
            send_sem=first_send.at[0],
            recv_sem=first_recv.at[0],
            device_id={"gz": owner(s)},
            device_id_type=MESH,
        )

    def first_all():
        part = gathered.at[0 : ngz - 1]
        return pltpu.make_async_remote_copy(
            src_ref=part,
            dst_ref=part,
            send_sem=first_send.at[0],
            recv_sem=first_recv.at[0],
            device_id={"gz": lax.rem(gz + 1, ngz)},
            device_id_type=MESH,
        )

    def project(group):
        rows = result[span(group)].reshape(members * cells, length)
        product = dot3(split(rows), (east_parts[0], east_parts[1]))
        for i in range(members):
            s = group * members + i
            part = product[i * cells : (i + 1) * cells]

            @pl.when(gz == owner(s))
            def _(s=s, part=part):
                gathered[owner(s)] = part

            @pl.when(gz != owner(s))
            def _(s=s, part=part):
                first[s] = part
                first_copy(s).start()

    store = pltpu.make_async_copy(result, next_hbm, load_sem.at[3])

    if fused:
        piece = chunk_ranks * width
        few = chunk_ranks * own
        parts = ranks_z // chunk_ranks // chunks
        block = parts * piece
        out = parts * few

        mine = gz // 2 + lax.rem(gz, 2) * (species // 2)

        def room(way, n):
            return gy + n < ngy if way else gy >= n

        def line_copy(way, d, chunk, held):
            origin = gy - held if way else gy + held
            part = second.at[origin, chunk * block : (chunk + 1) * block]
            return pltpu.make_async_remote_copy(
                src_ref=part,
                dst_ref=part,
                send_sem=second_send.at[way, d - 1],
                recv_sem=second_recv.at[way, d - 1, chunk],
                device_id={"gy": gy + d - held if way else gy + held - d},
                device_id_type=MESH,
            )

        def line_arrival(way, d, chunk):
            origin = gy - d if way else gy + d
            part = second.at[origin, chunk * block : (chunk + 1) * block]
            return pltpu.make_async_remote_copy(
                src_ref=part,
                dst_ref=part,
                send_sem=second_send.at[way, d - 1],
                recv_sem=second_recv.at[way, d - 1, chunk],
                device_id={"gy": other[3 - way]},
                device_id_type=MESH,
            )

        def each_own(chunk, act):
            for d in range(1, ngy):
                for way in range(2):
                    if d != 2:

                        @pl.when(room(way, d))
                        def _(way=way, d=d):
                            act(line_copy(way, d, chunk, 0))

        def each_relayed(way, chunk, act):
            @pl.when(jnp.logical_and(room(1 - way, 1), room(way, 1)))
            def _():
                act(line_copy(way, 2, chunk, 1))

        def start(copy):
            copy.start()

        def lines_sent():
            for way in range(2):
                for d in range(1, ngy):
                    leaves = room(way, d)
                    if d == 2:
                        leaves = jnp.logical_and(room(1 - way, 1), room(way, 1))

                    @pl.when(leaves)
                    def _(way=way, d=d):
                        part = second.at[gy]
                        pltpu.make_async_remote_copy(
                            src_ref=part,
                            dst_ref=part,
                            send_sem=second_send.at[way, d - 1],
                            recv_sem=second_recv.at[way, d - 1, 0],
                            device_id={"gy": other[2 + way]},
                            device_id_type=MESH,
                        ).wait_send()

        def third_copy(k, chunk):
            peer = lax.rem(gz + k, ngz)
            rows = slice(chunk * out, (chunk + 1) * out)
            return pltpu.make_async_remote_copy(
                src_ref=slabs.at[peer, rows],
                dst_ref=core_hbm.at[mine, rows],
                send_sem=third_send.at[0],
                recv_sem=third_recv.at[chunk],
                device_id={"gz": peer},
                device_id_type=MESH,
            )

        def third_all(rows, chunk):
            return pltpu.make_async_remote_copy(
                src_ref=slabs.at[0 : ngz - 1, rows],
                dst_ref=core_hbm.at[0 : ngz - 1, rows],
                send_sem=third_send.at[0],
                recv_sem=third_recv.at[chunk],
                device_id={"gz": lax.rem(gz + 1, ngz)},
                device_id_type=MESH,
            )

        def contract():
            first_all().wait_recv()
            slab = split(gathered[...].reshape(ngz * cells, ranks_x))
            for chunk in range(chunks):
                rows = slice(chunk * block, (chunk + 1) * block)
                second[gy, rows] = dot3((up_parts[0, rows], up_parts[1, rows]), slab)
                if chunk < ahead:
                    each_own(chunk, start)

        for group in range(groups):
            wait_halos(1, group)
            each_member(group, lambda s: fix(result, 1, s))
            project(group)
        store.start()
        contract()
        def await_line(d, chunk):
            for way in range(2):

                @pl.when(room(1 - way, d))
                def _(way=way):
                    line_arrival(way, d, chunk).wait_recv()

        def open_line(chunk):
            await_line(1, chunk)
            for way in range(2):
                each_relayed(way, chunk, start)

        def finish(chunk):
            for d in range(2, ngy):
                await_line(d, chunk)
            for part in range(parts):
                lines = slice(chunk * block + part * piece, chunk * block + (part + 1) * piece)
                rows = slice(chunk * out + part * few, chunk * out + (part + 1) * few)
                terms = second[:, lines, :].reshape(ngy * piece, ranks_x)
                product = dot3((north_parts[0], north_parts[1]), split(terms))
                slabs[:, rows, :] = product.reshape(ngz, few, ranks_x)
            for k in range(1, ngz):
                third_copy(k, chunk).start()

        for chunk in range(chunks):
            open_line(chunk)
            if chunk + ahead < chunks:
                each_own(chunk + ahead, start)
            if chunk >= behind:
                finish(chunk - behind)
        drain()
        store.wait()
        first_all().wait_send()
        for chunk in range(chunks - behind, chunks):
            finish(chunk)
        keep = pltpu.make_async_copy(slabs.at[gz], core_hbm.at[mine], load_sem.at[0])
        keep.start()
        lines_sent()
        keep.wait()
        for chunk in range(chunks):
            third_all(slice(chunk * out, (chunk + 1) * out), chunk).wait_recv()
        third_all(slice(0, chunks * out), 0).wait_send()
    else:
        for group in range(groups):
            wait_halos(1, group)
            each_member(group, lambda s: fix(result, 1, s))
        store.start()
        store.wait()
        drain()


def deliver_kernel(a_in, b_in, a_out, b_out, sems):
    copies = [
        pltpu.make_async_copy(a_in, a_out, sems.at[0]),
        pltpu.make_async_copy(b_in, b_out, sems.at[1]),
    ]
    for copy in copies:
        copy.start()
    for copy in copies:
        copy.wait()


def deliver(a, b):
    return pl.pallas_call(
        deliver_kernel,
        out_shape=[jax.ShapeDtypeStruct(x.shape, x.dtype) for x in (a, b)],
        in_specs=[pl.BlockSpec(memory_space=pl.ANY)] * 2,
        out_specs=[pl.BlockSpec(memory_space=pltpu.HBM)] * 2,
        scratch_shapes=[pltpu.SemaphoreType.DMA((2,))],
        compiler_params=pltpu.CompilerParams(vmem_limit_bytes=1 << 20),
        name="deliver",
    )(a, b)


def local(ngz, ngy, *args):
    u, t, d, a, b, m, e, n, up = args
    species, depth, width, length = u.shape
    ranks_x, ranks_y, ranks_z = e.shape[1], n.shape[1], up.shape[1]
    fused = species == ngz and species % 2 == 0 and ranks_z % (chunk_ranks * chunks) == 0 and ranks_y % ngz == 0
    fused = fused and chunk_ranks * (ranks_y // ngz) % 8 == 0
    anywhere = pl.BlockSpec(memory_space=pl.ANY)
    apart = pl.BlockSpec(memory_space=pltpu.HBM)
    packs = 2 * depth // width
    groups = most_groups if species % most_groups == 0 else 1
    outputs = [jax.ShapeDtypeStruct(u.shape, f32)]
    padded = (species, depth + 4, width, length)
    scratch = [
        pltpu.VMEM(padded, f32),
        pltpu.VMEM(padded, f32),
        pltpu.VMEM(u.shape, f32),
        pltpu.VMEM(u.shape, f32),
        pltpu.VMEM(t.shape, f32),
        pltpu.VMEM((2, 2, species, 2, width, length), f32),
        pltpu.VMEM((2, 2, species, packs, width, length), f32),
        pltpu.VMEM((2, 2, species, packs, width, length), f32),
        pltpu.SMEM(d.shape, f32),
        pltpu.SMEM(a.shape, f32),
        pltpu.SMEM(b.shape, f32),
        pltpu.SMEM(m.shape, f32),
        pltpu.SemaphoreType.DMA((10,)),
        pltpu.SemaphoreType.DMA((groups,)),
        pltpu.SemaphoreType.DMA((2, 4)),
        pltpu.SemaphoreType.DMA((2, 4, groups)),
    ]
    if fused:
        own = ranks_y // ngz
        cells = depth * width
        outputs.append(jax.ShapeDtypeStruct((species, ranks_z * own, ranks_x), f32))
        scratch += [
            pltpu.VMEM((length, ranks_x), f32),
            pltpu.VMEM(n.shape, f32),
            pltpu.VMEM(up.shape[::-1], f32),
            pltpu.VMEM((species, cells, ranks_x), f32),
            pltpu.VMEM((ngz, cells, ranks_x), f32),
            pltpu.VMEM((ngy, ranks_z * width, ranks_x), f32),
            pltpu.VMEM((ngz, ranks_z * own, ranks_x), f32),
            pltpu.VMEM((2, length, ranks_x), jnp.bfloat16),
            pltpu.VMEM((2, ranks_z * width, ngz * cells), jnp.bfloat16),
            pltpu.VMEM((2, ngz * chunk_ranks * own, ngy * chunk_ranks * width), jnp.bfloat16),
            pltpu.SemaphoreType.DMA((1,)),
            pltpu.SemaphoreType.DMA((1,)),
            pltpu.SemaphoreType.DMA((2, ngy - 1)),
            pltpu.SemaphoreType.DMA((2, ngy - 1, chunks)),
            pltpu.SemaphoreType.DMA((1,)),
            pltpu.SemaphoreType.DMA((chunks,)),
        ]
    outs = pl.pallas_call(
        functools.partial(kernel, ngz, ngy, fused),
        out_shape=outputs,
        in_specs=[apart] * 9,
        out_specs=[anywhere] * len(outputs),
        scratch_shapes=scratch,
        compiler_params=pltpu.CompilerParams(
            collective_id=0, has_side_effects=True, vmem_limit_bytes=48 << 20
        ),
        name="heun_step",
    )(*[pltpu.with_memory_space_constraint(x, pltpu.HBM) for x in (u, t, d, a, b, m, e, n, up.T)])
    if fused:
        outs = deliver(*outs)
        return outs[0], outs[1].reshape(species, ranks_z, own, ranks_x)
    species_next = outs[0]
    projected = jnp.einsum("szyx,xr->szyr", species_next, e, precision=HIGHEST)
    rows = lax.dynamic_slice_in_dim(n, lax.axis_index("gy") * width, width, 0)
    projected = jnp.einsum("szyr,yq->szqr", projected, rows, precision=HIGHEST)
    partial = jnp.einsum(
        "szqr,zp->spqr",
        lax.all_to_all(projected, "gz", split_axis=2, concat_axis=1, tiled=True),
        up,
        precision=HIGHEST,
    )
    return species_next, lax.psum(partial, "gy")


def solution(mesh):
    return jax.shard_map(
        functools.partial(local, mesh.shape["gz"], mesh.shape["gy"]),
        mesh=mesh,
        in_specs=(
            P(None, "gz", "gy", None),
            P("gz", "gy", None),
            P(),
            P(),
            P(),
            P(),
            P(),
            P(),
            P(),
        ),
        out_specs=(P(None, "gz", "gy", None), P(None, None, "gz", None)),
        check_vma=False,
    )
```

```python
import functools

import jax
import jax.numpy as jnp
from jax import lax
from jax.experimental import pallas as pl
from jax.experimental.pallas import tpu as pltpu
from jax.sharding import PartitionSpec as P

time_step = 0.1
chunk_ranks = 8
chunks = 4
ahead = 4
behind = 3
most_groups = 4
MESH = pl.DeviceIdType.MESH
HIGHEST = lax.Precision.HIGHEST
f32 = jnp.float32


def iota(shape, dim):
    return lax.broadcasted_iota(jnp.int32, shape, dim)


def dot(a, b, dims=(((1,), (0,)), ((), ()))):
    return lax.dot_general(a, b, dims, precision=HIGHEST, preferred_element_type=f32)


def split(x):
    top = x.astype(jnp.bfloat16)
    return top, (x - top.astype(f32)).astype(jnp.bfloat16)


def dot3(a, b):
    (a1, a2), (b1, b2) = a, b
    small = jnp.dot(a1, b2, preferred_element_type=f32)
    small += jnp.dot(a2, b1, preferred_element_type=f32)
    return small + jnp.dot(a1, b1, preferred_element_type=f32)


def kernel(ngz, ngy, fused, *refs):
    (
        u_hbm,
        t_hbm,
        d_hbm,
        a_hbm,
        b_hbm,
        m_hbm,
        e_hbm,
        n_hbm,
        up_hbm,
        next_hbm,
    ) = refs[:10]
    rest = refs[10:]
    if fused:
        core_hbm, rest = rest[0], rest[1:]
    (
        field,
        half,
        rate,
        result,
        thermal,
        zhalo,
        yhalo,
        ysend,
        d_ref,
        a_ref,
        b_ref,
        m_ref,
        load_sem,
        field_sem,
        halo_send,
        halo_recv,
    ) = rest[:16]
    if fused:
        (
            east,
            n_ref,
            up_ref,
            first,
            gathered,
            second,
            slabs,
            east_parts,
            up_parts,
            north_parts,
            first_send,
            first_recv,
            second_send,
            second_recv,
            third_send,
            third_recv,
        ) = rest[16:]

    species, depth, width, length = u_hbm.shape
    gz = lax.axis_index("gz")
    gy = lax.axis_index("gy")
    groups = halo_recv.shape[2]
    has = [gz > 0, gz < ngz - 1, gy > 0, gy < ngy - 1]
    names = ["gz", "gz", "gy", "gy"]
    other = [gz - 1, gz + 1, gy - 1, gy + 1]

    barrier = pltpu.get_barrier_semaphore()
    if fused:
        for k in range(1, ngz):
            pl.semaphore_signal(
                barrier, inc=1, device_id={"gz": lax.rem(gz + k, ngz)}, device_id_type=MESH
            )
        for k in range(1, ngy):
            pl.semaphore_signal(
                barrier, inc=1, device_id={"gy": lax.rem(gy + k, ngy)}, device_id_type=MESH
            )
    partners = () if fused else (0, 1, 2, 3)
    for side in partners:

        @pl.when(has[side])
        def _(side=side):
            pl.semaphore_signal(
                barrier, inc=1, device_id={names[side]: other[side]}, device_id_type=MESH
            )

    load_t = pltpu.make_async_copy(t_hbm, thermal, load_sem.at[1])
    small = [
        pltpu.make_async_copy(src, dst, load_sem.at[5 + i])
        for i, (src, dst) in enumerate(
            ((d_hbm, d_ref), (a_hbm, a_ref), (b_hbm, b_ref), (m_hbm, m_ref))
        )
    ]
    load_u = [
        pltpu.make_async_copy(
            u_hbm.at[lo : lo + species // groups],
            field.at[lo : lo + species // groups, 2 : 2 + depth],
            field_sem.at[group],
        )
        for group in range(groups)
        for lo in [group * (species // groups)]
    ]
    for copy in load_u:
        copy.start()
    for copy in small:
        copy.start()
    load_t.start()
    if fused:
        load_e = pltpu.make_async_copy(e_hbm, east, load_sem.at[2])
        load_n = pltpu.make_async_copy(n_hbm, n_ref, load_sem.at[9])
        load_up = pltpu.make_async_copy(up_hbm, up_ref, load_sem.at[4])
        for copy in (load_e, load_n, load_up):
            copy.start()

    row = iota((width, length), 0)
    lane = iota((width, length), 1)
    per = width // 2
    packs = depth // per

    def weight(s, stage):
        return d_ref[s] * (time_step / 12.0 * (0.5 if stage else 1.0))

    members = species // groups

    def each_member(group, step):
        def body(s, carry):
            step(s)
            return carry

        lax.fori_loop(group * members, (group + 1) * members, body, 0)

    def span(group):
        return slice(group * members, (group + 1) * members)

    def pack_rows(source, stage, s):
        first_gain = jnp.where(row == 0, 16.0, 0.0)
        last_gain = jnp.where(row == width - 1, 16.0, 0.0)

        k = weight(s, stage)
        for group in range(packs):
            up = jnp.zeros((width, length), f32)
            down = jnp.zeros((width, length), f32)
            for i in range(per):
                v = source[s, 2 + group * per + i] * k
                rising = first_gain * pltpu.roll(v, 1, 0) - pltpu.roll(v, 2, 0)
                falling = last_gain * pltpu.roll(v, width - 1, 0) - pltpu.roll(
                    v, width - 2, 0
                )
                here = jnp.logical_and(row >= 2 * i, row < 2 * i + 2)
                if i:
                    rising = pltpu.roll(rising, 2 * i, 0)
                falling = pltpu.roll(falling, (2 * i + 2) % width, 0) if i < per - 1 else falling
                up = jnp.where(here, rising, up)
                down = jnp.where(here, falling, down)
            ysend[stage, 0, s, group] = down
            ysend[stage, 1, s, group] = up

    def halo_copy(stage, side, group):
        who = span(group)
        if side < 2:
            start = 0 if side == 0 else depth - 2
            if stage == 0:
                src = u_hbm.at[who, start : start + 2]
            else:
                src = half.at[who, 2 + start : 4 + start]
            dst = zhalo.at[stage, 1 - side, who]
        else:
            src = ysend.at[stage, side - 2, who]
            dst = yhalo.at[stage, 3 - side, who]
        opposite = side ^ 1
        return pltpu.make_async_remote_copy(
            src_ref=src,
            dst_ref=dst,
            send_sem=halo_send.at[stage, side],
            recv_sem=halo_recv.at[stage, opposite, group],
            device_id={names[side]: other[side]},
            device_id_type=MESH,
        )

    def arrived(stage, side, group):
        who = span(group)
        dst = zhalo.at[stage, side, who] if side < 2 else yhalo.at[stage, side - 2, who]
        return pltpu.make_async_remote_copy(
            src_ref=dst,
            dst_ref=dst,
            send_sem=halo_send.at[stage, side],
            recv_sem=halo_recv.at[stage, side, group],
            device_id={names[side]: other[side]},
            device_id_type=MESH,
        )

    def send_halos(stage, sides, group):
        for side in sides:

            @pl.when(has[side])
            def _(side=side):
                halo_copy(stage, side, group).start()

    def wait_halos(stage, group):
        for side in range(4):

            @pl.when(has[side])
            def _(side=side):
                arrived(stage, side, group).wait_recv()

    def drain():
        for stage in range(2):
            for side in range(4):

                @pl.when(has[side])
                def _(stage=stage, side=side):
                    sent = zhalo.at[stage, side] if side < 2 else ysend.at[stage, side - 2]
                    pltpu.make_async_remote_copy(
                        src_ref=sent,
                        dst_ref=sent,
                        send_sem=halo_send.at[stage, side],
                        recv_sem=halo_recv.at[stage, side, 0],
                        device_id={names[side]: other[side]},
                        device_id_type=MESH,
                    ).wait_send()

    def local_pass(source, target, stage):
        offset = 0 if stage else 2
        gain = 0.5 if stage else 1.0

        def body(z, carry):
            for s in range(species):
                c = source[s, z + 2]
                near = source[s, z + 1] + source[s, z + 3]
                far = source[s, z] + source[s, z + 4]
                near += jnp.where(row >= 1, pltpu.roll(c, 1, 0), 0.0)
                near += jnp.where(row < width - 1, pltpu.roll(c, width - 1, 0), 0.0)
                far += jnp.where(row >= 2, pltpu.roll(c, 2, 0), 0.0)
                far += jnp.where(row < width - 2, pltpu.roll(c, width - 2, 0), 0.0)
                near += jnp.where(lane >= 1, pltpu.roll(c, 1, 1), 0.0)
                near += jnp.where(lane < length - 1, pltpu.roll(c, length - 1, 1), 0.0)
                far += jnp.where(lane >= 2, pltpu.roll(c, 2, 1), 0.0)
                far += jnp.where(lane < length - 2, pltpu.roll(c, length - 2, 1), 0.0)
                total = weight(s, stage) * (16.0 * near - far - 90.0 * c)
                if stage:
                    total += 0.5 * (c + field[s, z + 2])
                else:
                    total += c
                target[s, z + offset] = total
            for tile in range(0, length, 128):
                part = pl.ds(tile, 128)
                turnover = [
                    (rate[t, z, :, part] * source[t, z + 2, :, part]) * (gain * time_step)
                    for t in range(species)
                ]
                for s in range(species):
                    total = target[s, z + offset, :, part] - turnover[s]
                    for t in range(species):
                        total += m_ref[s, t] * turnover[t]
                    target[s, z + offset, :, part] = total
            return carry

        lax.fori_loop(0, depth, body, 0)

    def fix(target, stage, s):
        offset = 0 if stage else 2

        k = weight(s, stage)
        add = {}
        below, above = zhalo[stage, 0, s], zhalo[stage, 1, s]
        add[0] = k * (16.0 * below[1] - below[0])
        add[1] = -k * below[1]
        add[depth - 1] = k * (16.0 * above[0] - above[1])
        add[depth - 2] = -k * above[0]
        for group in range(packs):
            low, high = yhalo[stage, 0, s, group], yhalo[stage, 1, s, group]
            for i in range(per):
                z = group * per + i
                shift = (width - 2 * i) % width
                value = target[s, z + offset]
                value += jnp.where(row < 2, pltpu.roll(low, shift, 0) if shift else low, 0.0)
                shift = (2 * width - 2 - 2 * i) % width
                value += jnp.where(
                    row >= width - 2, pltpu.roll(high, shift, 0) if shift else high, 0.0
                )
                if z in add:
                    value += add[z]
                target[s, z + offset] = value

    if fused:
        pl.semaphore_wait(barrier, ngz + ngy - 2)
    for side in partners:

        @pl.when(has[side])
        def _():
            pl.semaphore_wait(barrier, 1)

    for group in range(groups):
        send_halos(0, (0, 1), group)
    for copy in small:
        copy.wait()
    for group in range(groups):
        load_u[group].wait()
        each_member(group, lambda s: pack_rows(field, 0, s))
        send_halos(0, (2, 3), group)

    zeros = jnp.zeros((species, 2, width, length), f32)
    for buffer in (field, half):
        buffer[:, 0:2] = zeros
        buffer[:, 2 + depth : 4 + depth] = zeros
    for side in range(2):

        @pl.when(jnp.logical_not(has[side]))
        def _(side=side):
            for stage in range(2):
                zhalo[stage, side] = zeros

        @pl.when(jnp.logical_not(has[2 + side]))
        def _(side=side):
            for stage in range(2):
                yhalo[stage, side] = jnp.zeros(yhalo.shape[2:], f32)

    load_t.wait()

    def rates(z, carry):
        inverse = 1.0 / thermal[z]
        for s in range(species):
            rate[s, z] = a_ref[s] * jnp.exp(-b_ref[s] * inverse)
        return carry

    lax.fori_loop(0, depth, rates, 0)
    local_pass(field, half, 0)

    if fused:
        load_n.wait()
        load_up.wait()
        load_e.wait()
        ranks_z = up_ref.shape[0]
        ranks_y = n_ref.shape[1]
        ranks_x = east.shape[1]
        own = ranks_y // ngz
        cells = depth * width
        for i, part in enumerate(split(east[...])):
            east_parts[i] = part
        rows, columns = up_parts.shape[1:]
        spread = dot(
            (iota((rows, ranks_z), 0) // width == iota((rows, ranks_z), 1)).astype(f32),
            up_ref[...],
        )
        heights = up_ref.shape[1]
        spread = dot(
            spread,
            (iota((heights, columns), 0) == iota((heights, columns), 1) // width).astype(f32),
        )
        spread = jnp.where(
            iota((rows, columns), 0) % width == iota((rows, columns), 1) % width, spread, 0.0
        )
        for i, part in enumerate(split(spread)):
            up_parts[i] = part
        rows, columns = north_parts.shape[1:]
        line = iota((rows, ranks_y), 0)
        pick = (line // (chunk_ranks * own)) * own + line % own == iota((rows, ranks_y), 1)
        spread = dot(pick.astype(f32), n_ref[...], (((1,), (1,)), ((), ())))
        widths = n_ref.shape[0]
        line = iota((widths, columns), 1)
        pick = (line // (chunk_ranks * width)) * width + line % width == iota((widths, columns), 0)
        spread = dot(spread, pick.astype(f32))
        spread = jnp.where(
            (iota((rows, columns), 0) // own) % chunk_ranks == (iota((rows, columns), 1) // width) % chunk_ranks,
            spread,
            0.0,
        )
        for i, part in enumerate(split(spread)):
            north_parts[i] = part

    for group in range(groups):
        wait_halos(0, group)

        each_member(group, lambda s: fix(half, 0, s))
        send_halos(1, (0, 1), group)
        each_member(group, lambda s: pack_rows(half, 1, s))
        send_halos(1, (2, 3), group)
    local_pass(half, result, 1)

    def owner(s):
        return s * 2 % species + 1 - s * 2 // species

    def first_copy(s):
        return pltpu.make_async_remote_copy(
            src_ref=first.at[s],
            dst_ref=gathered.at[gz],
            send_sem=first_send.at[0],
            recv_sem=first_recv.at[0],
            device_id={"gz": owner(s)},
            device_id_type=MESH,
        )

    def first_all():
        part = gathered.at[0 : ngz - 1]
        return pltpu.make_async_remote_copy(
            src_ref=part,
            dst_ref=part,
            send_sem=first_send.at[0],
            recv_sem=first_recv.at[0],
            device_id={"gz": lax.rem(gz + 1, ngz)},
            device_id_type=MESH,
        )

    def project(group):
        rows = result[span(group)].reshape(members * cells, length)
        product = dot3(split(rows), (east_parts[0], east_parts[1]))
        for i in range(members):
            s = group * members + i
            part = product[i * cells : (i + 1) * cells]

            @pl.when(gz == owner(s))
            def _(s=s, part=part):
                gathered[owner(s)] = part

            @pl.when(gz != owner(s))
            def _(s=s, part=part):
                first[s] = part
                first_copy(s).start()

    store = pltpu.make_async_copy(result, next_hbm, load_sem.at[3])

    if fused:
        piece = chunk_ranks * width
        few = chunk_ranks * own
        parts = ranks_z // chunk_ranks // chunks
        block = parts * piece
        out = parts * few

        mine = gz // 2 + (1 - lax.rem(gz, 2)) * (species // 2)

        def room(way, n):
            return gy + n < ngy if way else gy >= n

        def line_copy(way, d, chunk, held):
            origin = gy - held if way else gy + held
            part = second.at[origin, chunk * block : (chunk + 1) * block]
            return pltpu.make_async_remote_copy(
                src_ref=part,
                dst_ref=part,
                send_sem=second_send.at[way, d - 1],
                recv_sem=second_recv.at[way, d - 1, chunk],
                device_id={"gy": gy + d - held if way else gy + held - d},
                device_id_type=MESH,
            )

        def line_arrival(way, d, chunk):
            origin = gy - d if way else gy + d
            part = second.at[origin, chunk * block : (chunk + 1) * block]
            return pltpu.make_async_remote_copy(
                src_ref=part,
                dst_ref=part,
                send_sem=second_send.at[way, d - 1],
                recv_sem=second_recv.at[way, d - 1, chunk],
                device_id={"gy": other[3 - way]},
                device_id_type=MESH,
            )

        def each_own(chunk, act):
            for d in range(1, ngy):
                for way in range(2):
                    if d != 2:

                        @pl.when(room(way, d))
                        def _(way=way, d=d):
                            act(line_copy(way, d, chunk, 0))

        def each_relayed(way, chunk, act):
            @pl.when(jnp.logical_and(room(1 - way, 1), room(way, 1)))
            def _():
                act(line_copy(way, 2, chunk, 1))

        def start(copy):
            copy.start()

        def lines_sent():
            for way in range(2):
                for d in range(1, ngy):
                    leaves = room(way, d)
                    if d == 2:
                        leaves = jnp.logical_and(room(1 - way, 1), room(way, 1))

                    @pl.when(leaves)
                    def _(way=way, d=d):
                        part = second.at[gy]
                        pltpu.make_async_remote_copy(
                            src_ref=part,
                            dst_ref=part,
                            send_sem=second_send.at[way, d - 1],
                            recv_sem=second_recv.at[way, d - 1, 0],
                            device_id={"gy": other[2 + way]},
                            device_id_type=MESH,
                        ).wait_send()

        def third_copy(k, chunk):
            peer = lax.rem(gz + k, ngz)
            rows = slice(chunk * out, (chunk + 1) * out)
            return pltpu.make_async_remote_copy(
                src_ref=slabs.at[peer, rows],
                dst_ref=core_hbm.at[mine, rows],
                send_sem=third_send.at[0],
                recv_sem=third_recv.at[chunk],
                device_id={"gz": peer},
                device_id_type=MESH,
            )

        def third_all(rows, chunk):
            return pltpu.make_async_remote_copy(
                src_ref=slabs.at[0 : ngz - 1, rows],
                dst_ref=core_hbm.at[0 : ngz - 1, rows],
                send_sem=third_send.at[0],
                recv_sem=third_recv.at[chunk],
                device_id={"gz": lax.rem(gz + 1, ngz)},
                device_id_type=MESH,
            )

        def contract():
            first_all().wait_recv()
            slab = split(gathered[...].reshape(ngz * cells, ranks_x))
            for chunk in range(chunks):
                rows = slice(chunk * block, (chunk + 1) * block)
                second[gy, rows] = dot3((up_parts[0, rows], up_parts[1, rows]), slab)
                if chunk < ahead:
                    each_own(chunk, start)

        for group in range(groups):
            wait_halos(1, group)
            each_member(group, lambda s: fix(result, 1, s))
            project(group)
        contract()
        def await_line(d, chunk):
            for way in range(2):

                @pl.when(room(1 - way, d))
                def _(way=way):
                    line_arrival(way, d, chunk).wait_recv()

        def open_line(chunk):
            await_line(1, chunk)
            for way in range(2):
                each_relayed(way, chunk, start)

        def finish(chunk):
            for d in range(2, ngy):
                await_line(d, chunk)
            for part in range(parts):
                lines = slice(chunk * block + part * piece, chunk * block + (part + 1) * piece)
                rows = slice(chunk * out + part * few, chunk * out + (part + 1) * few)
                terms = second[:, lines, :].reshape(ngy * piece, ranks_x)
                product = dot3((north_parts[0], north_parts[1]), split(terms))
                slabs[:, rows, :] = product.reshape(ngz, few, ranks_x)
            for k in range(1, ngz):
                third_copy(k, chunk).start()

        for chunk in range(chunks):
            open_line(chunk)
            if chunk == 0:
                store.start()
            if chunk + ahead < chunks:
                each_own(chunk + ahead, start)
            if chunk >= behind:
                finish(chunk - behind)
        drain()
        store.wait()
        first_all().wait_send()
        for chunk in range(chunks - behind, chunks):
            finish(chunk)
        keep = pltpu.make_async_copy(slabs.at[gz], core_hbm.at[mine], load_sem.at[0])
        keep.start()
        lines_sent()
        keep.wait()
        for chunk in range(chunks):
            third_all(slice(chunk * out, (chunk + 1) * out), chunk).wait_recv()
        third_all(slice(0, chunks * out), 0).wait_send()
    else:
        for group in range(groups):
            wait_halos(1, group)
            each_member(group, lambda s: fix(result, 1, s))
        store.start()
        store.wait()
        drain()


def deliver_kernel(a_in, b_in, a_out, b_out, sems):
    copies = [
        pltpu.make_async_copy(a_in, a_out, sems.at[0]),
        pltpu.make_async_copy(b_in, b_out, sems.at[1]),
    ]
    for copy in copies:
        copy.start()
    for copy in copies:
        copy.wait()


def deliver(a, b):
    return pl.pallas_call(
        deliver_kernel,
        out_shape=[jax.ShapeDtypeStruct(x.shape, x.dtype) for x in (a, b)],
        in_specs=[pl.BlockSpec(memory_space=pl.ANY)] * 2,
        out_specs=[pl.BlockSpec(memory_space=pltpu.HBM)] * 2,
        scratch_shapes=[pltpu.SemaphoreType.DMA((2,))],
        compiler_params=pltpu.CompilerParams(vmem_limit_bytes=1 << 20),
        name="deliver",
    )(a, b)


def local(ngz, ngy, *args):
    u, t, d, a, b, m, e, n, up = args
    species, depth, width, length = u.shape
    ranks_x, ranks_y, ranks_z = e.shape[1], n.shape[1], up.shape[1]
    fused = species == ngz and species % 2 == 0 and ranks_z % (chunk_ranks * chunks) == 0 and ranks_y % ngz == 0
    fused = fused and chunk_ranks * (ranks_y // ngz) % 8 == 0
    anywhere = pl.BlockSpec(memory_space=pl.ANY)
    apart = pl.BlockSpec(memory_space=pltpu.HBM)
    packs = 2 * depth // width
    groups = most_groups if species % most_groups == 0 else 1
    outputs = [jax.ShapeDtypeStruct(u.shape, f32)]
    padded = (species, depth + 4, width, length)
    scratch = [
        pltpu.VMEM(padded, f32),
        pltpu.VMEM(padded, f32),
        pltpu.VMEM(u.shape, f32),
        pltpu.VMEM(u.shape, f32),
        pltpu.VMEM(t.shape, f32),
        pltpu.VMEM((2, 2, species, 2, width, length), f32),
        pltpu.VMEM((2, 2, species, packs, width, length), f32),
        pltpu.VMEM((2, 2, species, packs, width, length), f32),
        pltpu.SMEM(d.shape, f32),
        pltpu.SMEM(a.shape, f32),
        pltpu.SMEM(b.shape, f32),
        pltpu.SMEM(m.shape, f32),
        pltpu.SemaphoreType.DMA((10,)),
        pltpu.SemaphoreType.DMA((groups,)),
        pltpu.SemaphoreType.DMA((2, 4)),
        pltpu.SemaphoreType.DMA((2, 4, groups)),
    ]
    if fused:
        own = ranks_y // ngz
        cells = depth * width
        outputs.append(jax.ShapeDtypeStruct((species, ranks_z * own, ranks_x), f32))
        scratch += [
            pltpu.VMEM((length, ranks_x), f32),
            pltpu.VMEM(n.shape, f32),
            pltpu.VMEM(up.shape[::-1], f32),
            pltpu.VMEM((species, cells, ranks_x), f32),
            pltpu.VMEM((ngz, cells, ranks_x), f32),
            pltpu.VMEM((ngy, ranks_z * width, ranks_x), f32),
            pltpu.VMEM((ngz, ranks_z * own, ranks_x), f32),
            pltpu.VMEM((2, length, ranks_x), jnp.bfloat16),
            pltpu.VMEM((2, ranks_z * width, ngz * cells), jnp.bfloat16),
            pltpu.VMEM((2, ngz * chunk_ranks * own, ngy * chunk_ranks * width), jnp.bfloat16),
            pltpu.SemaphoreType.DMA((1,)),
            pltpu.SemaphoreType.DMA((1,)),
            pltpu.SemaphoreType.DMA((2, ngy - 1)),
            pltpu.SemaphoreType.DMA((2, ngy - 1, chunks)),
            pltpu.SemaphoreType.DMA((1,)),
            pltpu.SemaphoreType.DMA((chunks,)),
        ]
    outs = pl.pallas_call(
        functools.partial(kernel, ngz, ngy, fused),
        out_shape=outputs,
        in_specs=[apart] * 9,
        out_specs=[anywhere] * len(outputs),
        scratch_shapes=scratch,
        compiler_params=pltpu.CompilerParams(
            collective_id=0, has_side_effects=True, vmem_limit_bytes=48 << 20
        ),
        name="heun_step",
    )(*[pltpu.with_memory_space_constraint(x, pltpu.HBM) for x in (u, t, d, a, b, m, e, n, up.T)])
    if fused:
        outs = deliver(*outs)
        return outs[0], outs[1].reshape(species, ranks_z, own, ranks_x)
    species_next = outs[0]
    projected = jnp.einsum("szyx,xr->szyr", species_next, e, precision=HIGHEST)
    rows = lax.dynamic_slice_in_dim(n, lax.axis_index("gy") * width, width, 0)
    projected = jnp.einsum("szyr,yq->szqr", projected, rows, precision=HIGHEST)
    partial = jnp.einsum(
        "szqr,zp->spqr",
        lax.all_to_all(projected, "gz", split_axis=2, concat_axis=1, tiled=True),
        up,
        precision=HIGHEST,
    )
    return species_next, lax.psum(partial, "gy")


def solution(mesh):
    return jax.shard_map(
        functools.partial(local, mesh.shape["gz"], mesh.shape["gy"]),
        mesh=mesh,
        in_specs=(
            P(None, "gz", "gy", None),
            P("gz", "gy", None),
            P(),
            P(),
            P(),
            P(),
            P(),
            P(),
            P(),
        ),
        out_specs=(P(None, "gz", "gy", None), P(None, None, "gz", None)),
        check_vma=False,
    )
```

```python
import functools

import jax
import jax.numpy as jnp
from jax import lax
from jax.experimental import pallas as pl
from jax.experimental.pallas import tpu as pltpu
from jax.sharding import PartitionSpec as P

time_step = 0.1
chunk_ranks = 8
chunks = 4
ahead = 4
behind = 3
most_groups = 4
MESH = pl.DeviceIdType.MESH
HIGHEST = lax.Precision.HIGHEST
f32 = jnp.float32


def iota(shape, dim):
    return lax.broadcasted_iota(jnp.int32, shape, dim)


def dot(a, b, dims=(((1,), (0,)), ((), ()))):
    return lax.dot_general(a, b, dims, precision=HIGHEST, preferred_element_type=f32)


def split(x):
    top = x.astype(jnp.bfloat16)
    return top, (x - top.astype(f32)).astype(jnp.bfloat16)


def dot3(a, b):
    (a1, a2), (b1, b2) = a, b
    small = jnp.dot(a1, b2, preferred_element_type=f32)
    small += jnp.dot(a2, b1, preferred_element_type=f32)
    return small + jnp.dot(a1, b1, preferred_element_type=f32)


def kernel(ngz, ngy, fused, *refs):
    (
        u_hbm,
        t_hbm,
        d_hbm,
        a_hbm,
        b_hbm,
        m_hbm,
        e_hbm,
        n_hbm,
        up_hbm,
        next_hbm,
    ) = refs[:10]
    rest = refs[10:]
    if fused:
        core_hbm, rest = rest[0], rest[1:]
    (
        field,
        half,
        rate,
        result,
        thermal,
        zhalo,
        yhalo,
        ysend,
        d_ref,
        a_ref,
        b_ref,
        m_ref,
        load_sem,
        field_sem,
        halo_send,
        halo_recv,
    ) = rest[:16]
    if fused:
        (
            east,
            n_ref,
            up_ref,
            first,
            gathered,
            second,
            slabs,
            east_parts,
            up_parts,
            north_parts,
            first_send,
            first_recv,
            second_send,
            second_recv,
            third_send,
            third_recv,
        ) = rest[16:]

    species, depth, width, length = u_hbm.shape
    gz = lax.axis_index("gz")
    gy = lax.axis_index("gy")
    groups = halo_recv.shape[2]
    has = [gz > 0, gz < ngz - 1, gy > 0, gy < ngy - 1]
    names = ["gz", "gz", "gy", "gy"]
    other = [gz - 1, gz + 1, gy - 1, gy + 1]

    barrier = pltpu.get_barrier_semaphore()
    if fused:
        for k in range(1, ngz):
            pl.semaphore_signal(
                barrier, inc=1, device_id={"gz": lax.rem(gz + k, ngz)}, device_id_type=MESH
            )
        for k in range(1, ngy):
            pl.semaphore_signal(
                barrier, inc=1, device_id={"gy": lax.rem(gy + k, ngy)}, device_id_type=MESH
            )
    partners = () if fused else (0, 1, 2, 3)
    for side in partners:

        @pl.when(has[side])
        def _(side=side):
            pl.semaphore_signal(
                barrier, inc=1, device_id={names[side]: other[side]}, device_id_type=MESH
            )

    load_t = pltpu.make_async_copy(t_hbm, thermal, load_sem.at[1])
    small = [
        pltpu.make_async_copy(src, dst, load_sem.at[5 + i])
        for i, (src, dst) in enumerate(
            ((d_hbm, d_ref), (a_hbm, a_ref), (b_hbm, b_ref), (m_hbm, m_ref))
        )
    ]
    load_u = [
        pltpu.make_async_copy(
            u_hbm.at[lo : lo + species // groups],
            field.at[lo : lo + species // groups, 2 : 2 + depth],
            field_sem.at[group],
        )
        for group in range(groups)
        for lo in [group * (species // groups)]
    ]
    for copy in load_u:
        copy.start()
    for copy in small:
        copy.start()
    load_t.start()
    if fused:
        load_e = pltpu.make_async_copy(e_hbm, east, load_sem.at[2])
        load_n = pltpu.make_async_copy(n_hbm, n_ref, load_sem.at[9])
        load_up = pltpu.make_async_copy(up_hbm, up_ref, load_sem.at[4])
        for copy in (load_e, load_n, load_up):
            copy.start()

    row = iota((width, length), 0)
    lane = iota((width, length), 1)
    per = width // 2
    packs = depth // per

    def weight(s, stage):
        return d_ref[s] * (time_step / 12.0 * (0.5 if stage else 1.0))

    members = species // groups

    def each_member(group, step):
        def body(s, carry):
            step(s)
            return carry

        lax.fori_loop(group * members, (group + 1) * members, body, 0)

    def span(group):
        return slice(group * members, (group + 1) * members)

    def pack_rows(source, stage, s):
        first_gain = jnp.where(row == 0, 16.0, 0.0)
        last_gain = jnp.where(row == width - 1, 16.0, 0.0)

        k = weight(s, stage)
        for group in range(packs):
            up = jnp.zeros((width, length), f32)
            down = jnp.zeros((width, length), f32)
            for i in range(per):
                v = source[s, 2 + group * per + i] * k
                rising = first_gain * pltpu.roll(v, 1, 0) - pltpu.roll(v, 2, 0)
                falling = last_gain * pltpu.roll(v, width - 1, 0) - pltpu.roll(
                    v, width - 2, 0
                )
                here = jnp.logical_and(row >= 2 * i, row < 2 * i + 2)
                if i:
                    rising = pltpu.roll(rising, 2 * i, 0)
                falling = pltpu.roll(falling, (2 * i + 2) % width, 0) if i < per - 1 else falling
                up = jnp.where(here, rising, up)
                down = jnp.where(here, falling, down)
            ysend[stage, 0, s, group] = down
            ysend[stage, 1, s, group] = up

    def halo_copy(stage, side, group):
        who = span(group)
        if side < 2:
            start = 0 if side == 0 else depth - 2
            if stage == 0:
                src = u_hbm.at[who, start : start + 2]
            else:
                src = half.at[who, 2 + start : 4 + start]
            dst = zhalo.at[stage, 1 - side, who]
        else:
            src = ysend.at[stage, side - 2, who]
            dst = yhalo.at[stage, 3 - side, who]
        opposite = side ^ 1
        return pltpu.make_async_remote_copy(
            src_ref=src,
            dst_ref=dst,
            send_sem=halo_send.at[stage, side],
            recv_sem=halo_recv.at[stage, opposite, group],
            device_id={names[side]: other[side]},
            device_id_type=MESH,
        )

    def arrived(stage, side, group):
        who = span(group)
        dst = zhalo.at[stage, side, who] if side < 2 else yhalo.at[stage, side - 2, who]
        return pltpu.make_async_remote_copy(
            src_ref=dst,
            dst_ref=dst,
            send_sem=halo_send.at[stage, side],
            recv_sem=halo_recv.at[stage, side, group],
            device_id={names[side]: other[side]},
            device_id_type=MESH,
        )

    def send_halos(stage, sides, group):
        for side in sides:

            @pl.when(has[side])
            def _(side=side):
                halo_copy(stage, side, group).start()

    def wait_halos(stage, group):
        for side in range(4):

            @pl.when(has[side])
            def _(side=side):
                arrived(stage, side, group).wait_recv()

    def drain():
        for stage in range(2):
            for side in range(4):

                @pl.when(has[side])
                def _(stage=stage, side=side):
                    sent = zhalo.at[stage, side] if side < 2 else ysend.at[stage, side - 2]
                    pltpu.make_async_remote_copy(
                        src_ref=sent,
                        dst_ref=sent,
                        send_sem=halo_send.at[stage, side],
                        recv_sem=halo_recv.at[stage, side, 0],
                        device_id={names[side]: other[side]},
                        device_id_type=MESH,
                    ).wait_send()

    def local_pass(source, target, stage):
        offset = 0 if stage else 2
        gain = 0.5 if stage else 1.0

        def body(z, carry):
            for s in range(species):
                c = source[s, z + 2]
                near = source[s, z + 1] + source[s, z + 3]
                far = source[s, z] + source[s, z + 4]
                near += jnp.where(row >= 1, pltpu.roll(c, 1, 0), 0.0)
                near += jnp.where(row < width - 1, pltpu.roll(c, width - 1, 0), 0.0)
                far += jnp.where(row >= 2, pltpu.roll(c, 2, 0), 0.0)
                far += jnp.where(row < width - 2, pltpu.roll(c, width - 2, 0), 0.0)
                near += jnp.where(lane >= 1, pltpu.roll(c, 1, 1), 0.0)
                near += jnp.where(lane < length - 1, pltpu.roll(c, length - 1, 1), 0.0)
                far += jnp.where(lane >= 2, pltpu.roll(c, 2, 1), 0.0)
                far += jnp.where(lane < length - 2, pltpu.roll(c, length - 2, 1), 0.0)
                total = weight(s, stage) * (16.0 * near - far - 90.0 * c)
                if stage:
                    total += 0.5 * (c + field[s, z + 2])
                else:
                    total += c
                target[s, z + offset] = total
            for tile in range(0, length, 128):
                part = pl.ds(tile, 128)
                turnover = [
                    (rate[t, z, :, part] * source[t, z + 2, :, part]) * (gain * time_step)
                    for t in range(species)
                ]
                for s in range(species):
                    total = target[s, z + offset, :, part] - turnover[s]
                    for t in range(species):
                        total += m_ref[s, t] * turnover[t]
                    target[s, z + offset, :, part] = total
            return carry

        lax.fori_loop(0, depth, body, 0)

    def fix(target, stage, s):
        offset = 0 if stage else 2

        k = weight(s, stage)
        add = {}
        below, above = zhalo[stage, 0, s], zhalo[stage, 1, s]
        add[0] = k * (16.0 * below[1] - below[0])
        add[1] = -k * below[1]
        add[depth - 1] = k * (16.0 * above[0] - above[1])
        add[depth - 2] = -k * above[0]
        for group in range(packs):
            low, high = yhalo[stage, 0, s, group], yhalo[stage, 1, s, group]
            for i in range(per):
                z = group * per + i
                shift = (width - 2 * i) % width
                value = target[s, z + offset]
                value += jnp.where(row < 2, pltpu.roll(low, shift, 0) if shift else low, 0.0)
                shift = (2 * width - 2 - 2 * i) % width
                value += jnp.where(
                    row >= width - 2, pltpu.roll(high, shift, 0) if shift else high, 0.0
                )
                if z in add:
                    value += add[z]
                target[s, z + offset] = value

    if fused:
        pl.semaphore_wait(barrier, ngz + ngy - 2)
    for side in partners:

        @pl.when(has[side])
        def _():
            pl.semaphore_wait(barrier, 1)

    for group in range(groups):
        send_halos(0, (0, 1), group)
    for copy in small:
        copy.wait()
    for group in range(groups):
        load_u[group].wait()
        each_member(group, lambda s: pack_rows(field, 0, s))
        send_halos(0, (2, 3), group)

    zeros = jnp.zeros((species, 2, width, length), f32)
    for buffer in (field, half):
        buffer[:, 0:2] = zeros
        buffer[:, 2 + depth : 4 + depth] = zeros
    for side in range(2):

        @pl.when(jnp.logical_not(has[side]))
        def _(side=side):
            for stage in range(2):
                zhalo[stage, side] = zeros

        @pl.when(jnp.logical_not(has[2 + side]))
        def _(side=side):
            for stage in range(2):
                yhalo[stage, side] = jnp.zeros(yhalo.shape[2:], f32)

    load_t.wait()

    def rates(z, carry):
        inverse = 1.0 / thermal[z]
        for s in range(species):
            rate[s, z] = a_ref[s] * jnp.exp(-b_ref[s] * inverse)
        return carry

    lax.fori_loop(0, depth, rates, 0)
    local_pass(field, half, 0)

    if fused:
        load_n.wait()
        load_up.wait()
        load_e.wait()
        ranks_z = up_ref.shape[0]
        ranks_y = n_ref.shape[1]
        ranks_x = east.shape[1]
        own = ranks_y // ngz
        cells = depth * width
        for i, part in enumerate(split(east[...])):
            east_parts[i] = part
        rows, columns = up_parts.shape[1:]
        spread = dot(
            (iota((rows, ranks_z), 0) // width == iota((rows, ranks_z), 1)).astype(f32),
            up_ref[...],
        )
        heights = up_ref.shape[1]
        spread = dot(
            spread,
            (iota((heights, columns), 0) == iota((heights, columns), 1) // width).astype(f32),
        )
        spread = jnp.where(
            iota((rows, columns), 0) % width == iota((rows, columns), 1) % width, spread, 0.0
        )
        for i, part in enumerate(split(spread)):
            up_parts[i] = part
        rows, columns = north_parts.shape[1:]
        line = iota((rows, ranks_y), 0)
        pick = (line // (chunk_ranks * own)) * own + line % own == iota((rows, ranks_y), 1)
        spread = dot(pick.astype(f32), n_ref[...], (((1,), (1,)), ((), ())))
        widths = n_ref.shape[0]
        line = iota((widths, columns), 1)
        pick = (line // (chunk_ranks * width)) * width + line % width == iota((widths, columns), 0)
        spread = dot(spread, pick.astype(f32))
        spread = jnp.where(
            (iota((rows, columns), 0) // own) % chunk_ranks == (iota((rows, columns), 1) // width) % chunk_ranks,
            spread,
            0.0,
        )
        for i, part in enumerate(split(spread)):
            north_parts[i] = part

    for group in range(groups):
        wait_halos(0, group)

        each_member(group, lambda s: fix(half, 0, s))
        send_halos(1, (0, 1), group)
        each_member(group, lambda s: pack_rows(half, 1, s))
        send_halos(1, (2, 3), group)
    local_pass(half, result, 1)

    def owner(s):
        return s * 2 % species + 1 - s * 2 // species

    def first_copy(s):
        return pltpu.make_async_remote_copy(
            src_ref=first.at[s],
            dst_ref=gathered.at[gz],
            send_sem=first_send.at[0],
            recv_sem=first_recv.at[0],
            device_id={"gz": owner(s)},
            device_id_type=MESH,
        )

    def first_all():
        part = gathered.at[0 : ngz - 1]
        return pltpu.make_async_remote_copy(
            src_ref=part,
            dst_ref=part,
            send_sem=first_send.at[0],
            recv_sem=first_recv.at[0],
            device_id={"gz": lax.rem(gz + 1, ngz)},
            device_id_type=MESH,
        )

    def project(group):
        rows = result[span(group)].reshape(members * cells, length)
        product = dot3(split(rows), (east_parts[0], east_parts[1]))
        for i in range(members):
            s = group * members + i
            part = product[i * cells : (i + 1) * cells]

            @pl.when(gz == owner(s))
            def _(s=s, part=part):
                gathered[owner(s)] = part

            @pl.when(gz != owner(s))
            def _(s=s, part=part):
                first[s] = part
                first_copy(s).start()

    store = pltpu.make_async_copy(result, next_hbm, load_sem.at[3])

    if fused:
        piece = chunk_ranks * width
        few = chunk_ranks * own
        parts = ranks_z // chunk_ranks // chunks
        block = parts * piece
        out = parts * few

        mine = gz // 2 + (1 - lax.rem(gz, 2)) * (species // 2)

        def room(way, n):
            return gy + n < ngy if way else gy >= n

        def line_copy(way, d, chunk, held):
            origin = gy - held if way else gy + held
            part = second.at[origin, chunk * block : (chunk + 1) * block]
            return pltpu.make_async_remote_copy(
                src_ref=part,
                dst_ref=part,
                send_sem=second_send.at[way, d - 1],
                recv_sem=second_recv.at[way, d - 1, chunk],
                device_id={"gy": gy + d - held if way else gy + held - d},
                device_id_type=MESH,
            )

        def line_arrival(way, d, chunk):
            origin = gy - d if way else gy + d
            part = second.at[origin, chunk * block : (chunk + 1) * block]
            return pltpu.make_async_remote_copy(
                src_ref=part,
                dst_ref=part,
                send_sem=second_send.at[way, d - 1],
                recv_sem=second_recv.at[way, d - 1, chunk],
                device_id={"gy": other[3 - way]},
                device_id_type=MESH,
            )

        def each_own(chunk, act):
            for d in range(1, ngy):
                for way in range(2):
                    if d != 2:

                        @pl.when(room(way, d))
                        def _(way=way, d=d):
                            act(line_copy(way, d, chunk, 0))

        def each_relayed(way, chunk, act):
            @pl.when(jnp.logical_and(room(1 - way, 1), room(way, 1)))
            def _():
                act(line_copy(way, 2, chunk, 1))

        def start(copy):
            copy.start()

        def lines_sent():
            for way in range(2):
                for d in range(1, ngy):
                    leaves = room(way, d)
                    if d == 2:
                        leaves = jnp.logical_and(room(1 - way, 1), room(way, 1))

                    @pl.when(leaves)
                    def _(way=way, d=d):
                        part = second.at[gy]
                        pltpu.make_async_remote_copy(
                            src_ref=part,
                            dst_ref=part,
                            send_sem=second_send.at[way, d - 1],
                            recv_sem=second_recv.at[way, d - 1, 0],
                            device_id={"gy": other[2 + way]},
                            device_id_type=MESH,
                        ).wait_send()

        def third_copy(k, chunk):
            peer = lax.rem(gz + k, ngz)
            rows = slice(chunk * out, (chunk + 1) * out)
            return pltpu.make_async_remote_copy(
                src_ref=slabs.at[peer, rows],
                dst_ref=core_hbm.at[mine, rows],
                send_sem=third_send.at[0],
                recv_sem=third_recv.at[0],
                device_id={"gz": peer},
                device_id_type=MESH,
            )

        def third_all(rows):
            return pltpu.make_async_remote_copy(
                src_ref=slabs.at[0 : ngz - 1, rows],
                dst_ref=core_hbm.at[0 : ngz - 1, rows],
                send_sem=third_send.at[0],
                recv_sem=third_recv.at[0],
                device_id={"gz": lax.rem(gz + 1, ngz)},
                device_id_type=MESH,
            )

        def contract():
            first_all().wait_recv()
            slab = split(gathered[...].reshape(ngz * cells, ranks_x))
            for chunk in range(chunks):
                rows = slice(chunk * block, (chunk + 1) * block)
                second[gy, rows] = dot3((up_parts[0, rows], up_parts[1, rows]), slab)
                if chunk < ahead:
                    each_own(chunk, start)

        for group in range(groups):
            wait_halos(1, group)
            each_member(group, lambda s: fix(result, 1, s))
            project(group)
        contract()
        def await_line(d, chunk):
            for way in range(2):

                @pl.when(room(1 - way, d))
                def _(way=way):
                    line_arrival(way, d, chunk).wait_recv()

        def open_line(chunk):
            await_line(1, chunk)
            for way in range(2):
                each_relayed(way, chunk, start)

        def finish(chunk):
            for d in range(2, ngy):
                await_line(d, chunk)
            for part in range(parts):
                lines = slice(chunk * block + part * piece, chunk * block + (part + 1) * piece)
                rows = slice(chunk * out + part * few, chunk * out + (part + 1) * few)
                terms = second[:, lines, :].reshape(ngy * piece, ranks_x)
                product = dot3((north_parts[0], north_parts[1]), split(terms))
                slabs[:, rows, :] = product.reshape(ngz, few, ranks_x)
            for k in range(1, ngz):
                third_copy(k, chunk).start()

        for chunk in range(chunks):
            open_line(chunk)
            if chunk == 0:
                store.start()
            if chunk + ahead < chunks:
                each_own(chunk + ahead, start)
            if chunk >= behind:
                finish(chunk - behind)
        drain()
        store.wait()
        first_all().wait_send()
        for chunk in range(chunks - behind, chunks):
            finish(chunk)
        keep = pltpu.make_async_copy(slabs.at[gz], core_hbm.at[mine], load_sem.at[0])
        keep.start()
        lines_sent()
        keep.wait()
        third_all(slice(0, chunks * out)).wait_recv()
        third_all(slice(0, chunks * out)).wait_send()
    else:
        for group in range(groups):
            wait_halos(1, group)
            each_member(group, lambda s: fix(result, 1, s))
        store.start()
        store.wait()
        drain()


def deliver_kernel(a_in, b_in, a_out, b_out, sems):
    copies = [
        pltpu.make_async_copy(a_in, a_out, sems.at[0]),
        pltpu.make_async_copy(b_in, b_out, sems.at[1]),
    ]
    for copy in copies:
        copy.start()
    for copy in copies:
        copy.wait()


def deliver(a, b):
    return pl.pallas_call(
        deliver_kernel,
        out_shape=[jax.ShapeDtypeStruct(x.shape, x.dtype) for x in (a, b)],
        in_specs=[pl.BlockSpec(memory_space=pl.ANY)] * 2,
        out_specs=[pl.BlockSpec(memory_space=pltpu.HBM)] * 2,
        scratch_shapes=[pltpu.SemaphoreType.DMA((2,))],
        compiler_params=pltpu.CompilerParams(vmem_limit_bytes=1 << 20),
        name="deliver",
    )(a, b)


def local(ngz, ngy, *args):
    u, t, d, a, b, m, e, n, up = args
    species, depth, width, length = u.shape
    ranks_x, ranks_y, ranks_z = e.shape[1], n.shape[1], up.shape[1]
    fused = species == ngz and species % 2 == 0 and ranks_z % (chunk_ranks * chunks) == 0 and ranks_y % ngz == 0
    fused = fused and chunk_ranks * (ranks_y // ngz) % 8 == 0
    anywhere = pl.BlockSpec(memory_space=pl.ANY)
    apart = pl.BlockSpec(memory_space=pltpu.HBM)
    packs = 2 * depth // width
    groups = most_groups if species % most_groups == 0 else 1
    outputs = [jax.ShapeDtypeStruct(u.shape, f32)]
    padded = (species, depth + 4, width, length)
    scratch = [
        pltpu.VMEM(padded, f32),
        pltpu.VMEM(padded, f32),
        pltpu.VMEM(u.shape, f32),
        pltpu.VMEM(u.shape, f32),
        pltpu.VMEM(t.shape, f32),
        pltpu.VMEM((2, 2, species, 2, width, length), f32),
        pltpu.VMEM((2, 2, species, packs, width, length), f32),
        pltpu.VMEM((2, 2, species, packs, width, length), f32),
        pltpu.SMEM(d.shape, f32),
        pltpu.SMEM(a.shape, f32),
        pltpu.SMEM(b.shape, f32),
        pltpu.SMEM(m.shape, f32),
        pltpu.SemaphoreType.DMA((10,)),
        pltpu.SemaphoreType.DMA((groups,)),
        pltpu.SemaphoreType.DMA((2, 4)),
        pltpu.SemaphoreType.DMA((2, 4, groups)),
    ]
    if fused:
        own = ranks_y // ngz
        cells = depth * width
        outputs.append(jax.ShapeDtypeStruct((species, ranks_z * own, ranks_x), f32))
        scratch += [
            pltpu.VMEM((length, ranks_x), f32),
            pltpu.VMEM(n.shape, f32),
            pltpu.VMEM(up.shape[::-1], f32),
            pltpu.VMEM((species, cells, ranks_x), f32),
            pltpu.VMEM((ngz, cells, ranks_x), f32),
            pltpu.VMEM((ngy, ranks_z * width, ranks_x), f32),
            pltpu.VMEM((ngz, ranks_z * own, ranks_x), f32),
            pltpu.VMEM((2, length, ranks_x), jnp.bfloat16),
            pltpu.VMEM((2, ranks_z * width, ngz * cells), jnp.bfloat16),
            pltpu.VMEM((2, ngz * chunk_ranks * own, ngy * chunk_ranks * width), jnp.bfloat16),
            pltpu.SemaphoreType.DMA((1,)),
            pltpu.SemaphoreType.DMA((1,)),
            pltpu.SemaphoreType.DMA((2, ngy - 1)),
            pltpu.SemaphoreType.DMA((2, ngy - 1, chunks)),
            pltpu.SemaphoreType.DMA((1,)),
            pltpu.SemaphoreType.DMA((1,)),
        ]
    outs = pl.pallas_call(
        functools.partial(kernel, ngz, ngy, fused),
        out_shape=outputs,
        in_specs=[apart] * 9,
        out_specs=[anywhere] * len(outputs),
        scratch_shapes=scratch,
        compiler_params=pltpu.CompilerParams(
            collective_id=0, has_side_effects=True, vmem_limit_bytes=48 << 20
        ),
        name="heun_step",
    )(*[pltpu.with_memory_space_constraint(x, pltpu.HBM) for x in (u, t, d, a, b, m, e, n, up.T)])
    if fused:
        outs = deliver(*outs)
        return outs[0], outs[1].reshape(species, ranks_z, own, ranks_x)
    species_next = outs[0]
    projected = jnp.einsum("szyx,xr->szyr", species_next, e, precision=HIGHEST)
    rows = lax.dynamic_slice_in_dim(n, lax.axis_index("gy") * width, width, 0)
    projected = jnp.einsum("szyr,yq->szqr", projected, rows, precision=HIGHEST)
    partial = jnp.einsum(
        "szqr,zp->spqr",
        lax.all_to_all(projected, "gz", split_axis=2, concat_axis=1, tiled=True),
        up,
        precision=HIGHEST,
    )
    return species_next, lax.psum(partial, "gy")


def solution(mesh):
    return jax.shard_map(
        functools.partial(local, mesh.shape["gz"], mesh.shape["gy"]),
        mesh=mesh,
        in_specs=(
            P(None, "gz", "gy", None),
            P("gz", "gy", None),
            P(),
            P(),
            P(),
            P(),
            P(),
            P(),
            P(),
        ),
        out_specs=(P(None, "gz", "gy", None), P(None, None, "gz", None)),
        check_vma=False,
    )
```

```python
import functools

import jax
import jax.numpy as jnp
from jax import lax
from jax.experimental import pallas as pl
from jax.experimental.pallas import tpu as pltpu
from jax.sharding import PartitionSpec as P

time_step = 0.1
chunk_ranks = 8
chunks = 4
ahead = 4
behind = 3
most_groups = 4
MESH = pl.DeviceIdType.MESH
HIGHEST = lax.Precision.HIGHEST
f32 = jnp.float32


def iota(shape, dim):
    return lax.broadcasted_iota(jnp.int32, shape, dim)


def dot(a, b, dims=(((1,), (0,)), ((), ()))):
    return lax.dot_general(a, b, dims, precision=HIGHEST, preferred_element_type=f32)


def split(x):
    top = x.astype(jnp.bfloat16)
    return top, (x - top.astype(f32)).astype(jnp.bfloat16)


def dot3(a, b):
    (a1, a2), (b1, b2) = a, b
    small = jnp.dot(a1, b2, preferred_element_type=f32)
    small += jnp.dot(a2, b1, preferred_element_type=f32)
    return small + jnp.dot(a1, b1, preferred_element_type=f32)


def kernel(ngz, ngy, fused, *refs):
    (
        u_hbm,
        t_hbm,
        d_hbm,
        a_hbm,
        b_hbm,
        m_hbm,
        e_hbm,
        n_hbm,
        up_hbm,
        next_hbm,
    ) = refs[:10]
    rest = refs[10:]
    if fused:
        core_hbm, rest = rest[0], rest[1:]
    (
        field,
        half,
        rate,
        result,
        thermal,
        zhalo,
        yhalo,
        ysend,
        d_ref,
        a_ref,
        b_ref,
        m_ref,
        load_sem,
        field_sem,
        halo_send,
        halo_recv,
    ) = rest[:16]
    if fused:
        (
            east,
            n_ref,
            up_ref,
            first,
            gathered,
            second,
            slabs,
            east_parts,
            up_parts,
            north_parts,
            first_send,
            first_recv,
            second_send,
            second_recv,
            third_send,
            third_recv,
        ) = rest[16:]

    species, depth, width, length = u_hbm.shape
    gz = lax.axis_index("gz")
    gy = lax.axis_index("gy")
    groups = halo_recv.shape[2]
    has = [gz > 0, gz < ngz - 1, gy > 0, gy < ngy - 1]
    names = ["gz", "gz", "gy", "gy"]
    other = [gz - 1, gz + 1, gy - 1, gy + 1]

    barrier = pltpu.get_barrier_semaphore()
    if fused:
        for k in range(1, ngz):
            pl.semaphore_signal(
                barrier, inc=1, device_id={"gz": lax.rem(gz + k, ngz)}, device_id_type=MESH
            )
        for k in range(1, ngy):
            pl.semaphore_signal(
                barrier, inc=1, device_id={"gy": lax.rem(gy + k, ngy)}, device_id_type=MESH
            )
    partners = () if fused else (0, 1, 2, 3)
    for side in partners:

        @pl.when(has[side])
        def _(side=side):
            pl.semaphore_signal(
                barrier, inc=1, device_id={names[side]: other[side]}, device_id_type=MESH
            )

    load_t = pltpu.make_async_copy(t_hbm, thermal, load_sem.at[1])
    small = [
        pltpu.make_async_copy(src, dst, load_sem.at[5 + i])
        for i, (src, dst) in enumerate(
            ((d_hbm, d_ref), (a_hbm, a_ref), (b_hbm, b_ref), (m_hbm, m_ref))
        )
    ]
    load_u = [
        pltpu.make_async_copy(
            u_hbm.at[lo : lo + species // groups],
            field.at[lo : lo + species // groups, 2 : 2 + depth],
            field_sem.at[group],
        )
        for group in range(groups)
        for lo in [group * (species // groups)]
    ]
    for copy in load_u:
        copy.start()
    for copy in small:
        copy.start()
    load_t.start()
    if fused:
        load_e = pltpu.make_async_copy(e_hbm, east, load_sem.at[2])
        load_n = pltpu.make_async_copy(n_hbm, n_ref, load_sem.at[9])
        load_up = pltpu.make_async_copy(up_hbm, up_ref, load_sem.at[4])
        for copy in (load_e, load_n, load_up):
            copy.start()

    row = iota((width, length), 0)
    lane = iota((width, length), 1)
    per = width // 2
    packs = depth // per

    def weight(s, stage):
        return d_ref[s] * (time_step / 12.0 * (0.5 if stage else 1.0))

    members = species // groups

    def each_member(group, step):
        def body(s, carry):
            step(s)
            return carry

        lax.fori_loop(group * members, (group + 1) * members, body, 0)

    def span(group):
        return slice(group * members, (group + 1) * members)

    def pack_rows(source, stage, s):
        first_gain = jnp.where(row == 0, 16.0, 0.0)
        last_gain = jnp.where(row == width - 1, 16.0, 0.0)

        k = weight(s, stage)
        for group in range(packs):
            up = jnp.zeros((width, length), f32)
            down = jnp.zeros((width, length), f32)
            for i in range(per):
                v = source[s, 2 + group * per + i] * k
                rising = first_gain * pltpu.roll(v, 1, 0) - pltpu.roll(v, 2, 0)
                falling = last_gain * pltpu.roll(v, width - 1, 0) - pltpu.roll(
                    v, width - 2, 0
                )
                here = jnp.logical_and(row >= 2 * i, row < 2 * i + 2)
                if i:
                    rising = pltpu.roll(rising, 2 * i, 0)
                falling = pltpu.roll(falling, (2 * i + 2) % width, 0) if i < per - 1 else falling
                up = jnp.where(here, rising, up)
                down = jnp.where(here, falling, down)
            ysend[stage, 0, s, group] = down
            ysend[stage, 1, s, group] = up

    def halo_copy(stage, side, group):
        who = span(group)
        if side < 2:
            start = 0 if side == 0 else depth - 2
            if stage == 0:
                src = u_hbm.at[who, start : start + 2]
            else:
                src = half.at[who, 2 + start : 4 + start]
            dst = zhalo.at[stage, 1 - side, who]
        else:
            src = ysend.at[stage, side - 2, who]
            dst = yhalo.at[stage, 3 - side, who]
        opposite = side ^ 1
        return pltpu.make_async_remote_copy(
            src_ref=src,
            dst_ref=dst,
            send_sem=halo_send.at[stage, side],
            recv_sem=halo_recv.at[stage, opposite, group],
            device_id={names[side]: other[side]},
            device_id_type=MESH,
        )

    def arrived(stage, side, group):
        who = span(group)
        dst = zhalo.at[stage, side, who] if side < 2 else yhalo.at[stage, side - 2, who]
        return pltpu.make_async_remote_copy(
            src_ref=dst,
            dst_ref=dst,
            send_sem=halo_send.at[stage, side],
            recv_sem=halo_recv.at[stage, side, group],
            device_id={names[side]: other[side]},
            device_id_type=MESH,
        )

    def send_halos(stage, sides, group):
        for side in sides:

            @pl.when(has[side])
            def _(side=side):
                halo_copy(stage, side, group).start()

    def wait_halos(stage, group):
        for side in range(4):

            @pl.when(has[side])
            def _(side=side):
                arrived(stage, side, group).wait_recv()

    def drain():
        for stage in range(2):
            for side in range(4):

                @pl.when(has[side])
                def _(stage=stage, side=side):
                    sent = zhalo.at[stage, side] if side < 2 else ysend.at[stage, side - 2]
                    pltpu.make_async_remote_copy(
                        src_ref=sent,
                        dst_ref=sent,
                        send_sem=halo_send.at[stage, side],
                        recv_sem=halo_recv.at[stage, side, 0],
                        device_id={names[side]: other[side]},
                        device_id_type=MESH,
                    ).wait_send()

    def local_pass(source, target, stage):
        offset = 0 if stage else 2
        gain = 0.5 if stage else 1.0

        def body(z, carry):
            for s in range(species):
                c = source[s, z + 2]
                near = source[s, z + 1] + source[s, z + 3]
                far = source[s, z] + source[s, z + 4]
                near += jnp.where(row >= 1, pltpu.roll(c, 1, 0), 0.0)
                near += jnp.where(row < width - 1, pltpu.roll(c, width - 1, 0), 0.0)
                far += jnp.where(row >= 2, pltpu.roll(c, 2, 0), 0.0)
                far += jnp.where(row < width - 2, pltpu.roll(c, width - 2, 0), 0.0)
                near += jnp.where(lane >= 1, pltpu.roll(c, 1, 1), 0.0)
                near += jnp.where(lane < length - 1, pltpu.roll(c, length - 1, 1), 0.0)
                far += jnp.where(lane >= 2, pltpu.roll(c, 2, 1), 0.0)
                far += jnp.where(lane < length - 2, pltpu.roll(c, length - 2, 1), 0.0)
                total = weight(s, stage) * (16.0 * near - far - 90.0 * c)
                if stage:
                    total += 0.5 * (c + field[s, z + 2])
                else:
                    total += c
                target[s, z + offset] = total
            for tile in range(0, length, 128):
                part = pl.ds(tile, 128)
                turnover = [
                    (rate[t, z, :, part] * source[t, z + 2, :, part]) * (gain * time_step)
                    for t in range(species)
                ]
                for s in range(species):
                    total = target[s, z + offset, :, part] - turnover[s]
                    for t in range(species):
                        total += m_ref[s, t] * turnover[t]
                    target[s, z + offset, :, part] = total
            return carry

        lax.fori_loop(0, depth, body, 0)

    def fix(target, stage, s):
        offset = 0 if stage else 2

        k = weight(s, stage)
        add = {}
        below, above = zhalo[stage, 0, s], zhalo[stage, 1, s]
        add[0] = k * (16.0 * below[1] - below[0])
        add[1] = -k * below[1]
        add[depth - 1] = k * (16.0 * above[0] - above[1])
        add[depth - 2] = -k * above[0]
        for group in range(packs):
            low, high = yhalo[stage, 0, s, group], yhalo[stage, 1, s, group]
            for i in range(per):
                z = group * per + i
                shift = (width - 2 * i) % width
                value = target[s, z + offset]
                value += jnp.where(row < 2, pltpu.roll(low, shift, 0) if shift else low, 0.0)
                shift = (2 * width - 2 - 2 * i) % width
                value += jnp.where(
                    row >= width - 2, pltpu.roll(high, shift, 0) if shift else high, 0.0
                )
                if z in add:
                    value += add[z]
                target[s, z + offset] = value

    if fused:
        pl.semaphore_wait(barrier, ngz + ngy - 2)
    for side in partners:

        @pl.when(has[side])
        def _():
            pl.semaphore_wait(barrier, 1)

    for group in range(groups):
        send_halos(0, (0, 1), group)
    for copy in small:
        copy.wait()
    for group in range(groups):
        load_u[group].wait()
        each_member(group, lambda s: pack_rows(field, 0, s))
        send_halos(0, (2, 3), group)

    zeros = jnp.zeros((species, 2, width, length), f32)
    for buffer in (field, half):
        buffer[:, 0:2] = zeros
        buffer[:, 2 + depth : 4 + depth] = zeros
    for side in range(2):

        @pl.when(jnp.logical_not(has[side]))
        def _(side=side):
            for stage in range(2):
                zhalo[stage, side] = zeros

        @pl.when(jnp.logical_not(has[2 + side]))
        def _(side=side):
            for stage in range(2):
                yhalo[stage, side] = jnp.zeros(yhalo.shape[2:], f32)

    load_t.wait()

    def rates(z, carry):
        inverse = 1.0 / thermal[z]
        for s in range(species):
            rate[s, z] = a_ref[s] * jnp.exp(-b_ref[s] * inverse)
        return carry

    lax.fori_loop(0, depth, rates, 0)
    local_pass(field, half, 0)

    if fused:
        load_n.wait()
        load_up.wait()
        load_e.wait()
        ranks_z = up_ref.shape[0]
        ranks_y = n_ref.shape[1]
        ranks_x = east.shape[1]
        own = ranks_y // ngz
        cells = depth * width
        for i, part in enumerate(split(east[...])):
            east_parts[i] = part
        rows, columns = up_parts.shape[1:]
        spread = dot(
            (iota((rows, ranks_z), 0) // width == iota((rows, ranks_z), 1)).astype(f32),
            up_ref[...],
        )
        heights = up_ref.shape[1]
        spread = dot(
            spread,
            (iota((heights, columns), 0) == iota((heights, columns), 1) // width).astype(f32),
        )
        spread = jnp.where(
            iota((rows, columns), 0) % width == iota((rows, columns), 1) % width, spread, 0.0
        )
        for i, part in enumerate(split(spread)):
            up_parts[i] = part
        rows, columns = north_parts.shape[1:]
        line = iota((rows, ranks_y), 0)
        pick = (line // (chunk_ranks * own)) * own + line % own == iota((rows, ranks_y), 1)
        spread = dot(pick.astype(f32), n_ref[...], (((1,), (1,)), ((), ())))
        widths = n_ref.shape[0]
        line = iota((widths, columns), 1)
        pick = (line // (chunk_ranks * width)) * width + line % width == iota((widths, columns), 0)
        spread = dot(spread, pick.astype(f32))
        spread = jnp.where(
            (iota((rows, columns), 0) // own) % chunk_ranks == (iota((rows, columns), 1) // width) % chunk_ranks,
            spread,
            0.0,
        )
        for i, part in enumerate(split(spread)):
            north_parts[i] = part

    for group in range(groups):
        wait_halos(0, group)

        each_member(group, lambda s: fix(half, 0, s))
        send_halos(1, (0, 1), group)
        each_member(group, lambda s: pack_rows(half, 1, s))
        send_halos(1, (2, 3), group)
    local_pass(half, result, 1)

    def owner(s):
        return s * 2 % species + 1 - s * 2 // species

    def first_copy(s):
        return pltpu.make_async_remote_copy(
            src_ref=first.at[s],
            dst_ref=gathered.at[gz],
            send_sem=first_send.at[0],
            recv_sem=first_recv.at[0],
            device_id={"gz": owner(s)},
            device_id_type=MESH,
        )

    def first_all():
        part = gathered.at[0 : ngz - 1]
        return pltpu.make_async_remote_copy(
            src_ref=part,
            dst_ref=part,
            send_sem=first_send.at[0],
            recv_sem=first_recv.at[0],
            device_id={"gz": lax.rem(gz + 1, ngz)},
            device_id_type=MESH,
        )

    def project(group):
        rows = result[span(group)].reshape(members * cells, length)
        product = dot3(split(rows), (east_parts[0], east_parts[1]))
        for i in range(members):
            s = group * members + i
            part = product[i * cells : (i + 1) * cells]

            @pl.when(gz == owner(s))
            def _(s=s, part=part):
                gathered[owner(s)] = part

            @pl.when(gz != owner(s))
            def _(s=s, part=part):
                first[s] = part
                first_copy(s).start()

    store = pltpu.make_async_copy(result, next_hbm, load_sem.at[3])

    if fused:
        piece = chunk_ranks * width
        few = chunk_ranks * own
        parts = ranks_z // chunk_ranks // chunks
        block = parts * piece
        out = parts * few

        mine = gz // 2 + (1 - lax.rem(gz, 2)) * (species // 2)

        def room(way, n):
            return gy + n < ngy if way else gy >= n

        def line_copy(way, d, chunk, held):
            origin = gy - held if way else gy + held
            part = second.at[origin, chunk * block : (chunk + 1) * block]
            return pltpu.make_async_remote_copy(
                src_ref=part,
                dst_ref=part,
                send_sem=second_send.at[way, d - 1],
                recv_sem=second_recv.at[way, d - 1, chunk],
                device_id={"gy": gy + d - held if way else gy + held - d},
                device_id_type=MESH,
            )

        def line_arrival(way, d, chunk):
            origin = gy - d if way else gy + d
            part = second.at[origin, chunk * block : (chunk + 1) * block]
            return pltpu.make_async_remote_copy(
                src_ref=part,
                dst_ref=part,
                send_sem=second_send.at[way, d - 1],
                recv_sem=second_recv.at[way, d - 1, chunk],
                device_id={"gy": other[3 - way]},
                device_id_type=MESH,
            )

        def each_own(chunk, act):
            for d in range(1, ngy):
                for way in range(2):
                    if d != 2:

                        @pl.when(room(way, d))
                        def _(way=way, d=d):
                            act(line_copy(way, d, chunk, 0))

        def each_relayed(way, chunk, act):
            @pl.when(jnp.logical_and(room(1 - way, 1), room(way, 1)))
            def _():
                act(line_copy(way, 2, chunk, 1))

        def start(copy):
            copy.start()

        def lines_sent():
            for way in range(2):
                for d in range(1, ngy):
                    leaves = room(way, d)
                    if d == 2:
                        leaves = jnp.logical_and(room(1 - way, 1), room(way, 1))

                    @pl.when(leaves)
                    def _(way=way, d=d):
                        part = second.at[gy]
                        pltpu.make_async_remote_copy(
                            src_ref=part,
                            dst_ref=part,
                            send_sem=second_send.at[way, d - 1],
                            recv_sem=second_recv.at[way, d - 1, 0],
                            device_id={"gy": other[2 + way]},
                            device_id_type=MESH,
                        ).wait_send()

        def partner(k):
            if ngz & (ngz - 1):
                return lax.rem(gz + k, ngz)
            bits = [1 << i for i in range(ngz.bit_length() - 1)]
            return sum(lax.rem(gz // bit + k // bit, 2) * bit for bit in bits)

        far_first = sorted(range(1, ngz), key=lambda k: -bin(k // 2).count('1'))

        def third_copy(k, chunk):
            peer = partner(k)
            rows = slice(chunk * out, (chunk + 1) * out)
            return pltpu.make_async_remote_copy(
                src_ref=slabs.at[peer, rows],
                dst_ref=core_hbm.at[mine, rows],
                send_sem=third_send.at[0],
                recv_sem=third_recv.at[0],
                device_id={"gz": peer},
                device_id_type=MESH,
            )

        def third_all(rows):
            return pltpu.make_async_remote_copy(
                src_ref=slabs.at[0 : ngz - 1, rows],
                dst_ref=core_hbm.at[0 : ngz - 1, rows],
                send_sem=third_send.at[0],
                recv_sem=third_recv.at[0],
                device_id={"gz": lax.rem(gz + 1, ngz)},
                device_id_type=MESH,
            )

        def contract():
            first_all().wait_recv()
            slab = split(gathered[...].reshape(ngz * cells, ranks_x))
            for chunk in range(chunks):
                rows = slice(chunk * block, (chunk + 1) * block)
                second[gy, rows] = dot3((up_parts[0, rows], up_parts[1, rows]), slab)
                if chunk < ahead:
                    each_own(chunk, start)

        for group in range(groups):
            wait_halos(1, group)
            each_member(group, lambda s: fix(result, 1, s))
            project(group)
        contract()
        def await_line(d, chunk):
            for way in range(2):

                @pl.when(room(1 - way, d))
                def _(way=way):
                    line_arrival(way, d, chunk).wait_recv()

        def open_line(chunk):
            await_line(1, chunk)
            for way in range(2):
                each_relayed(way, chunk, start)

        def finish(chunk):
            for d in range(2, ngy):
                await_line(d, chunk)
            for part in range(parts):
                lines = slice(chunk * block + part * piece, chunk * block + (part + 1) * piece)
                rows = slice(chunk * out + part * few, chunk * out + (part + 1) * few)
                terms = second[:, lines, :].reshape(ngy * piece, ranks_x)
                product = dot3((north_parts[0], north_parts[1]), split(terms))
                slabs[:, rows, :] = product.reshape(ngz, few, ranks_x)
            for k in far_first:
                third_copy(k, chunk).start()

        for chunk in range(chunks):
            open_line(chunk)
            if chunk == 0:
                store.start()
            if chunk + ahead < chunks:
                each_own(chunk + ahead, start)
            if chunk >= behind:
                finish(chunk - behind)
        drain()
        store.wait()
        first_all().wait_send()
        for chunk in range(chunks - behind, chunks):
            finish(chunk)
        keep = pltpu.make_async_copy(slabs.at[gz], core_hbm.at[mine], load_sem.at[0])
        keep.start()
        lines_sent()
        keep.wait()
        third_all(slice(0, chunks * out)).wait_recv()
        third_all(slice(0, chunks * out)).wait_send()
    else:
        for group in range(groups):
            wait_halos(1, group)
            each_member(group, lambda s: fix(result, 1, s))
        store.start()
        store.wait()
        drain()


def deliver_kernel(a_in, b_in, a_out, b_out, sems):
    copies = [
        pltpu.make_async_copy(a_in, a_out, sems.at[0]),
        pltpu.make_async_copy(b_in, b_out, sems.at[1]),
    ]
    for copy in copies:
        copy.start()
    for copy in copies:
        copy.wait()


def deliver(a, b):
    return pl.pallas_call(
        deliver_kernel,
        out_shape=[jax.ShapeDtypeStruct(x.shape, x.dtype) for x in (a, b)],
        in_specs=[pl.BlockSpec(memory_space=pl.ANY)] * 2,
        out_specs=[pl.BlockSpec(memory_space=pltpu.HBM)] * 2,
        scratch_shapes=[pltpu.SemaphoreType.DMA((2,))],
        compiler_params=pltpu.CompilerParams(vmem_limit_bytes=1 << 20),
        name="deliver",
    )(a, b)


def local(ngz, ngy, *args):
    u, t, d, a, b, m, e, n, up = args
    species, depth, width, length = u.shape
    ranks_x, ranks_y, ranks_z = e.shape[1], n.shape[1], up.shape[1]
    fused = species == ngz and species % 2 == 0 and ranks_z % (chunk_ranks * chunks) == 0 and ranks_y % ngz == 0
    fused = fused and chunk_ranks * (ranks_y // ngz) % 8 == 0
    anywhere = pl.BlockSpec(memory_space=pl.ANY)
    apart = pl.BlockSpec(memory_space=pltpu.HBM)
    packs = 2 * depth // width
    groups = most_groups if species % most_groups == 0 else 1
    outputs = [jax.ShapeDtypeStruct(u.shape, f32)]
    padded = (species, depth + 4, width, length)
    scratch = [
        pltpu.VMEM(padded, f32),
        pltpu.VMEM(padded, f32),
        pltpu.VMEM(u.shape, f32),
        pltpu.VMEM(u.shape, f32),
        pltpu.VMEM(t.shape, f32),
        pltpu.VMEM((2, 2, species, 2, width, length), f32),
        pltpu.VMEM((2, 2, species, packs, width, length), f32),
        pltpu.VMEM((2, 2, species, packs, width, length), f32),
        pltpu.SMEM(d.shape, f32),
        pltpu.SMEM(a.shape, f32),
        pltpu.SMEM(b.shape, f32),
        pltpu.SMEM(m.shape, f32),
        pltpu.SemaphoreType.DMA((10,)),
        pltpu.SemaphoreType.DMA((groups,)),
        pltpu.SemaphoreType.DMA((2, 4)),
        pltpu.SemaphoreType.DMA((2, 4, groups)),
    ]
    if fused:
        own = ranks_y // ngz
        cells = depth * width
        outputs.append(jax.ShapeDtypeStruct((species, ranks_z * own, ranks_x), f32))
        scratch += [
            pltpu.VMEM((length, ranks_x), f32),
            pltpu.VMEM(n.shape, f32),
            pltpu.VMEM(up.shape[::-1], f32),
            pltpu.VMEM((species, cells, ranks_x), f32),
            pltpu.VMEM((ngz, cells, ranks_x), f32),
            pltpu.VMEM((ngy, ranks_z * width, ranks_x), f32),
            pltpu.VMEM((ngz, ranks_z * own, ranks_x), f32),
            pltpu.VMEM((2, length, ranks_x), jnp.bfloat16),
            pltpu.VMEM((2, ranks_z * width, ngz * cells), jnp.bfloat16),
            pltpu.VMEM((2, ngz * chunk_ranks * own, ngy * chunk_ranks * width), jnp.bfloat16),
            pltpu.SemaphoreType.DMA((1,)),
            pltpu.SemaphoreType.DMA((1,)),
            pltpu.SemaphoreType.DMA((2, ngy - 1)),
            pltpu.SemaphoreType.DMA((2, ngy - 1, chunks)),
            pltpu.SemaphoreType.DMA((1,)),
            pltpu.SemaphoreType.DMA((1,)),
        ]
    outs = pl.pallas_call(
        functools.partial(kernel, ngz, ngy, fused),
        out_shape=outputs,
        in_specs=[apart] * 9,
        out_specs=[anywhere] * len(outputs),
        scratch_shapes=scratch,
        compiler_params=pltpu.CompilerParams(
            collective_id=0, has_side_effects=True, vmem_limit_bytes=48 << 20
        ),
        name="heun_step",
    )(*[pltpu.with_memory_space_constraint(x, pltpu.HBM) for x in (u, t, d, a, b, m, e, n, up.T)])
    if fused:
        outs = deliver(*outs)
        return outs[0], outs[1].reshape(species, ranks_z, own, ranks_x)
    species_next = outs[0]
    projected = jnp.einsum("szyx,xr->szyr", species_next, e, precision=HIGHEST)
    rows = lax.dynamic_slice_in_dim(n, lax.axis_index("gy") * width, width, 0)
    projected = jnp.einsum("szyr,yq->szqr", projected, rows, precision=HIGHEST)
    partial = jnp.einsum(
        "szqr,zp->spqr",
        lax.all_to_all(projected, "gz", split_axis=2, concat_axis=1, tiled=True),
        up,
        precision=HIGHEST,
    )
    return species_next, lax.psum(partial, "gy")


def solution(mesh):
    return jax.shard_map(
        functools.partial(local, mesh.shape["gz"], mesh.shape["gy"]),
        mesh=mesh,
        in_specs=(
            P(None, "gz", "gy", None),
            P("gz", "gy", None),
            P(),
            P(),
            P(),
            P(),
            P(),
            P(),
            P(),
        ),
        out_specs=(P(None, "gz", "gy", None), P(None, None, "gz", None)),
        check_vma=False,
    )
```
